32 devices in a mesh: dp: 16 (over z, y, core), mp: 2 (over x).
Axes of the slice: x: 2, y: 2, z: 4, core: 2. Of those that a mesh axis runs over, the one named last changes fastest.
Arguments:
- tokens_in: bfloat16 [4096, 2048], P(('dp', 'mp')), may hold values from -6 to 6
- teacher: bfloat16 [4096, 2048], P(('dp', 'mp')), may hold values from -6 to 6
- valid_mask: int32 [16, 256], P('dp', 'mp'), may hold values from 0 to 1, as said below
- group_of: int32 [16], replicated, may hold values from 0 to 1, as said below
- prompt_len: int32 [2], replicated, may hold values from 128 to 256
- ln1_gain: bfloat16 [2048], P('dp'), may hold values from 0.5 to 1.5
- ln1_bias: bfloat16 [2048], P('dp'), may hold values from -2 to 2
- w_query: bfloat16 [2048, 2048], P('dp', 'mp'), may hold values from -0.125 to 0.125
- w_key: bfloat16 [2048, 2048], P('dp', 'mp'), may hold values from -0.125 to 0.125
- w_value: bfloat16 [2048, 4096], P('dp', 'mp'), may hold values from -0.125 to 0.125
- w_gate: bfloat16 [2048, 4096], P('dp', 'mp'), may hold values from -0.125 to 0.125
- w_out: bfloat16 [2048, 4096], P('dp', 'mp'), may hold values from -0.1875 to 0.1875
- ln2_gain: bfloat16 [2048], P('dp'), may hold values from 0.5 to 1.5
- ln2_bias: bfloat16 [2048], P('dp'), may hold values from -2 to 2
- w_up: bfloat16 [2048, 4096], P('dp', 'mp'), may hold values from -0.125 to 0.125
- w_down: bfloat16 [2048, 4096], P('dp', 'mp'), may hold values from -0.125 to 0.125
Outputs:
- block_out: float32 [4096, 2048], P(('dp', 'mp'))
- grad_tokens: float32 [4096, 2048], P(('dp', 'mp'))
- loss: float32 [], replicated
- grad_ln1_gain: float32 [2048], P('dp')
- grad_ln1_bias: float32 [2048], P('dp')
- grad_w_query: float32 [2048, 2048], P('dp', 'mp')
- grad_w_key: float32 [2048, 2048], P('dp', 'mp')
- grad_w_value: float32 [2048, 4096], P('dp', 'mp')
- grad_w_gate: float32 [2048, 4096], P('dp', 'mp')
- grad_w_out: float32 [2048, 4096], P('dp', 'mp')
- grad_ln2_gain: float32 [2048], P('dp')
- grad_ln2_bias: float32 [2048], P('dp')
- grad_w_up: float32 [2048, 4096], P('dp', 'mp')
- grad_w_down: float32 [2048, 4096], P('dp', 'mp')
The draws below stay inside these ranges and needn't reach their ends.
Inputs may be any that keep to these rules, and one draw needn't show every extreme that they name: `valid_mask`: in each row the ones form a leading run of one or more positions, zeros follow. `group_of`: each group number is held by exactly 8 segments; a group's prompt is its lowest-numbered segment, the others are its continuations.
All inputs are finite; a program needn't handle non-finite values.
Results may differ from the reference program's by a relative error of at most 0.013.
Values may be sent and summed in bfloat16 or wider, within the bound.
A program may use at most 192 MiB of HBM per device.

```python
import math
import jax
import jax.numpy as jnp
from jax import lax

D = 2048
H = 8
DK = 256
DV = 512
FF = 4096
SEG = 256
GROUP = 8
NSEG = 16
NGROUP = 2
TOKENS = 4096


def draw_valid_mask(key, part):
    segment = jnp.arange(NSEG, dtype=jnp.int32)
    low_len = SEG // 3
    rising = low_len + (SEG - low_len) * segment // max(NSEG - 1, 1)
    jitter = jax.random.randint(key, (NSEG,), 0, SEG // 8 + 1, dtype=jnp.int32)
    length = jnp.maximum(rising - jitter, 1)
    return (jnp.arange(SEG, dtype=jnp.int32)[None, :] < length[:, None]).astype(jnp.int32)


def draw_group_of(key, part):
    shuffled = jax.random.permutation(key, NSEG)
    return (jnp.argsort(shuffled) // GROUP).astype(jnp.int32)


def block_levels(own_key, dims, pieces, low, high):
    level, own = 1.0, jax.random.fold_in(own_key, 6)
    for dim, blocks in pieces:
        draws = jnp.exp(jax.random.uniform(jax.random.fold_in(own, dim), (blocks,), jnp.float32, low / len(pieces), high / len(pieces)))
        level = level * jnp.repeat(draws, dims[dim] // blocks).reshape([-1 if axis == dim else 1 for axis in range(len(dims))])
    return level


def normal_values(own_key, shape, scale, bound, pieces=(), held_as=jnp.bfloat16):
    array = jax.random.normal(own_key, shape, jnp.float32) * scale
    if len(pieces) > 0:
        array = block_levels(own_key, shape, pieces, -0.22, 0.18) * array
    return jnp.clip(array, min=-bound, max=bound).astype(held_as)


def setup_inputs(seed: int = 0) -> dict:
    streams_of = jax.random.split(jax.random.key(seed), 17)
    tokens_in = normal_values(streams_of[0], (TOKENS, D), 1.0, 6.0, ((0, 32),))
    teacher = normal_values(streams_of[1], (TOKENS, D), 1.0, 6.0, ((0, 32),))
    valid_mask = draw_valid_mask(jax.random.fold_in(streams_of[16], 71), 0)
    group_of = draw_group_of(jax.random.fold_in(streams_of[16], 71), 0)
    prompt_len = jax.random.randint(streams_of[4], (NGROUP,), SEG // 2, SEG + 1).astype(jnp.int32)
    ln1_gain = jnp.clip(1.0 + 0.1 * jax.random.normal(streams_of[5], (D,), jnp.float32), 0.5, 1.5).astype(jnp.bfloat16)
    ln1_bias = normal_values(streams_of[6], (D,), 0.3, 2.0, ((0, 16),))
    w_query = normal_values(streams_of[7], (D, H * DK), D ** -0.5, 0.125, ((0, 16), (1, 2)))
    w_key = normal_values(streams_of[8], (D, H * DK), D ** -0.5, 0.125, ((0, 16), (1, 2)))
    w_value = normal_values(streams_of[9], (D, H * DV), D ** -0.5, 0.125, ((0, 16), (1, 2)))
    w_gate = normal_values(streams_of[10], (D, H * DV), D ** -0.5, 0.125, ((0, 16), (1, 2)))
    w_out = normal_values(streams_of[11], (D, H * DV), (H * DV // 4) ** -0.5, 0.1875, ((0, 16), (1, 2)))
    ln2_gain = jnp.clip(1.0 + 0.1 * jax.random.normal(streams_of[12], (D,), jnp.float32), 0.5, 1.5).astype(jnp.bfloat16)
    ln2_bias = normal_values(streams_of[13], (D,), 0.3, 2.0, ((0, 16),))
    w_up = normal_values(streams_of[14], (D, FF), D ** -0.5, 0.125, ((0, 16), (1, 2)))
    w_down = normal_values(streams_of[15], (D, FF), (FF // 2) ** -0.5, 0.125, ((0, 16), (1, 2)))
    return {"tokens_in": tokens_in, "teacher": teacher, "valid_mask": valid_mask, "group_of": group_of, "prompt_len": prompt_len, "ln1_gain": ln1_gain, "ln1_bias": ln1_bias, "w_query": w_query, "w_key": w_key, "w_value": w_value, "w_gate": w_gate, "w_out": w_out, "ln2_gain": ln2_gain, "ln2_bias": ln2_bias, "w_up": w_up, "w_down": w_down}


EPSILON = 1e-05
GROUP_EPSILON = 0.05
HIGHEST_ACCURACY = lax.Precision.HIGHEST

@jax.custom_vjp
def low(v):
    return lax.optimization_barrier(v.astype(jnp.bfloat16)).astype(jnp.float32)

@jax.custom_vjp
def low_back(v):
    return v

def low_keep(v):
    return (low(v), None)

def low_pass(kept, grad):
    return (grad,)

def back_keep(v):
    return (v, None)

def back_low(kept, grad):
    return (low(grad),)
low.defvjp(low_keep, low_pass)
low_back.defvjp(back_keep, back_low)

def norm_plain(values, floor_eps):
    center = lax.optimization_barrier(jnp.mean(values, axis=-1, keepdims=True))
    shifted = values - center
    inv_std = lax.rsqrt(lax.optimization_barrier(jnp.mean(shifted * shifted, axis=-1, keepdims=True)) + floor_eps)
    return shifted * inv_std

def layer_norm(values, gain_vec, bias_vec):
    return norm_plain(values, EPSILON) * gain_vec + bias_vec

def high_dot(first_op, second_op):
    return jnp.dot(first_op, second_op, precision=HIGHEST_ACCURACY)

def high_dot_t(first_op, second_op):
    return lax.dot_general(first_op, second_op, (((1,), (1,)), ((), ())), precision=HIGHEST_ACCURACY)

def xpos_tables(positions, direction):
    half_dim = DK // 2
    pair_index = jnp.arange(half_dim, dtype=jnp.float32)
    frequency = jnp.exp(-(2.0 * pair_index / DK) * math.log(10000.0))
    base_ratio = (2.0 * pair_index / DK + 0.4) / 1.4
    angles = positions[:, None] * frequency[None, :]
    factor = jnp.exp(direction * (positions[:, None] / 512.0) * jnp.log(base_ratio)[None, :])
    return (jnp.cos(angles), jnp.sin(angles), factor)

def rotate_pairs(values, cosine, sine_tab, factor):
    half_dim = values.shape[-1] // 2
    first_half = values[..., :half_dim]
    second = values[..., half_dim:]
    cosine = cosine[:, None, :]
    sine_tab = sine_tab[:, None, :]
    factor = factor[:, None, :]
    return jnp.concatenate([(first_half * cosine - second * sine_tab) * factor, (second * cosine + first_half * sine_tab) * factor], axis=-1)

def segment_layer(params, state_registry, inputs):
    gain_one, bias_one, w_query, w_key, w_value, w_gate, w_out, gain_two, bias_two, w_up, w_down = params
    seg_tokens, positions, state_weighting, continuation_factor, group_onehot, prompt_flag = inputs
    row_count = seg_tokens.shape[0]
    normed = low(layer_norm(seg_tokens, gain_one, bias_one))
    queries = low_back(high_dot(normed, w_query)).reshape(row_count, H, DK)
    keys_raw = low_back(high_dot(normed, w_key)).reshape(row_count, H, DK)
    reduced_values = low(low_back(high_dot(normed, w_value))).reshape(row_count, H, DV)
    gate_pre = low_back(high_dot(normed, w_gate))
    cosine, sine_tab, grow_fac = xpos_tables(positions, 1.0)
    _, _, shrink = xpos_tables(positions, -1.0)
    rotated_queries = low(rotate_pairs(queries, cosine, sine_tab, grow_fac) * DK ** (-0.5))
    rotated_keys = low(rotate_pairs(keys_raw, cosine, sine_tab, shrink))
    local_state = jnp.einsum('jld,jla->lda', rotated_keys * state_weighting[:, :, None], reduced_values, precision=HIGHEST_ACCURACY)
    state_low = low(low_back(local_state))
    state_registry = state_registry + prompt_flag * group_onehot[:, None, None, None] * state_low[None]
    state_lookup = jnp.einsum('b,bftm->ftm', group_onehot, state_registry, precision=HIGHEST_ACCURACY)
    log_decay = jnp.log(1.0 - 2.0 ** (-5.0 - jnp.arange(H, dtype=jnp.float32)))
    token_ids = jnp.arange(row_count, dtype=jnp.float32)
    distance = token_ids[:, None] - token_ids[None, :]
    decay_mat = jnp.where(distance[None] >= 0.0, jnp.exp(log_decay[:, None, None] * jnp.maximum(distance, 0.0)[None]), 0.0)
    scores = low_back(jnp.einsum('thk,nhk->htn', rotated_queries, rotated_keys, precision=HIGHEST_ACCURACY))
    weights_low = low(scores * decay_mat)
    retained_output = jnp.einsum('htn,nhv->thv', weights_low, reduced_values, precision=HIGHEST_ACCURACY)
    retained_output = retained_output + continuation_factor[:, :, None] * jnp.einsum('ozi,ziw->ozw', rotated_queries, state_lookup, precision=HIGHEST_ACCURACY)
    retained_output = low_back(retained_output)
    grouped = norm_plain(retained_output, GROUP_EPSILON)
    gated_out = low(jax.nn.silu(gate_pre).reshape(row_count, H, DV) * grouped).reshape(row_count, H * DV)
    attn_out = low_back(high_dot_t(gated_out, w_out))
    hidden_res = seg_tokens + attn_out
    normed_two = low(layer_norm(hidden_res, gain_two, bias_two))
    up_pre = low_back(high_dot(normed_two, w_up))
    up_act = low(jax.nn.gelu(up_pre, approximate=False))
    ffn_out = low_back(high_dot_t(up_act, w_down))
    return (state_registry, hidden_res + ffn_out)

def reference(tokens_in, teacher, valid_mask, group_of, prompt_len, ln1_gain, ln1_bias, w_query, w_key, w_value, w_gate, w_out, ln2_gain, ln2_bias, w_up, w_down):
    segment_ids = jnp.arange(NSEG, dtype=jnp.int32)
    same_group = group_of[:, None] == group_of[None, :]
    first_member = lax.optimization_barrier(jnp.min(jnp.where(same_group, segment_ids[None, :], NSEG), axis=1))
    is_prompt = first_member == segment_ids
    prompt_flag = is_prompt.astype(jnp.float32)
    group_match = group_of[:, None] == jnp.arange(NGROUP, dtype=jnp.int32)[None, :]
    group_onehot = group_match.astype(jnp.float32)
    prompt_size = lax.optimization_barrier(jnp.sum(jnp.where(group_match, prompt_len[None, :], 0), axis=1)).astype(jnp.int32)
    token_ids = jnp.arange(SEG, dtype=jnp.int32)
    offsets = jnp.where(is_prompt, 0, prompt_size)
    positions = (token_ids[None, :] + offsets[:, None]).astype(jnp.float32)
    log_decay = jnp.log(1.0 - 2.0 ** (-5.0 - jnp.arange(H, dtype=jnp.float32)))
    before_end = token_ids[None, :] < prompt_size[:, None]
    state_age = (prompt_size[:, None] - 1 - token_ids[None, :]).astype(jnp.float32)
    state_weighting = jnp.where((is_prompt[:, None] & before_end)[:, :, None], jnp.exp(log_decay[None, None, :] * jnp.maximum(state_age, 0.0)[:, :, None]), 0.0)
    continuation_factor = (1.0 - prompt_flag)[:, None, None] * jnp.exp(log_decay[None, None, :] * (token_ids.astype(jnp.float32) + 1.0)[None, :, None])
    loss_mask = valid_mask.astype(jnp.float32) * jnp.where(is_prompt[:, None], before_end, True).astype(jnp.float32)
    segment_order = jnp.argsort(1 - is_prompt.astype(jnp.int32), stable=True).astype(jnp.int32)
    inverse = jnp.argsort(segment_order, stable=True).astype(jnp.int32)
    params = (ln1_gain.astype(jnp.float32), ln1_bias.astype(jnp.float32), w_query.astype(jnp.float32), w_key.astype(jnp.float32), w_value.astype(jnp.float32), w_gate.astype(jnp.float32), w_out.astype(jnp.float32), ln2_gain.astype(jnp.float32), ln2_bias.astype(jnp.float32), w_up.astype(jnp.float32), w_down.astype(jnp.float32))

    def forward(token_rows, weights):
        segments = token_rows.reshape(NSEG, SEG, D)[segment_order]
        inputs = (segments, positions[segment_order], state_weighting[segment_order], continuation_factor[segment_order], group_onehot[segment_order], prompt_flag[segment_order])
        state_registry = jnp.zeros((NGROUP, H, DK, DV), jnp.float32)
        stepper = jax.checkpoint(lambda carried_forward, inner: segment_layer(weights, carried_forward, inner))
        _, outputs = lax.scan(stepper, state_registry, inputs)
        return outputs[inverse].reshape(NSEG * SEG, D)
    token_rows = tokens_in.astype(jnp.float32)
    block_out, pullback = jax.vjp(forward, token_rows, params)
    error_rows = block_out - teacher.astype(jnp.float32)
    mask_rows = loss_mask.reshape(NSEG * SEG)
    valid_count = jnp.sum(mask_rows)
    squared = jnp.sum(mask_rows[:, None] * error_rows * error_rows)
    grad_out = TOKENS / valid_count * mask_rows[:, None] * error_rows
    grad_tokens, grad_params = pullback(grad_out)
    loss_value = squared / (valid_count * D)
    return (block_out, grad_tokens, loss_value, grad_params[0], grad_params[1], grad_params[2], grad_params[3], grad_params[4], grad_params[5], grad_params[6], grad_params[7], grad_params[8], grad_params[9], grad_params[10])
```

```python
import math

import jax
import jax.numpy as jnp
from jax import lax
from jax.experimental import pallas as pl
from jax.experimental.pallas import tpu as pltpu
from jax.sharding import PartitionSpec as P

DK = 256
DV = 512


EPSILON = 1e-05
GROUP_EPSILON = 0.05


def norm_stats(values, floor_eps):
    center = jnp.mean(values, axis=-1, keepdims=True)
    shifted = values - center
    inv_std = lax.rsqrt(jnp.mean(shifted * shifted, axis=-1, keepdims=True) + floor_eps)
    return (shifted * inv_std, inv_std)


def norm_back(grad_in, normed, inv_std):
    mean_grad = jnp.mean(grad_in, axis=-1, keepdims=True)
    mean_proj = jnp.mean(grad_in * normed, axis=-1, keepdims=True)
    return (grad_in - mean_grad - normed * mean_proj) * inv_std


def xpos_tables(positions, direction):
    half_dim = DK // 2
    pair_index = jnp.arange(half_dim, dtype=jnp.float32)
    frequency = jnp.exp(-(2.0 * pair_index / DK) * math.log(10000.0))
    base_ratio = (2.0 * pair_index / DK + 0.4) / 1.4
    angles = positions[:, None] * frequency[None, :]
    factor = jnp.exp(direction * (positions[:, None] / 512.0) * jnp.log(base_ratio)[None, :])
    return (jnp.cos(angles), jnp.sin(angles), factor)


def rotate_pairs(values, cosine, sine_tab, factor):
    half_dim = values.shape[-1] // 2
    first_half = values[..., :half_dim]
    second = values[..., half_dim:]
    cosine = cosine[:, None, :]
    sine_tab = sine_tab[:, None, :]
    factor = factor[:, None, :]
    return jnp.concatenate(
        [
            (first_half * cosine - second * sine_tab) * factor,
            (second * cosine + first_half * sine_tab) * factor,
        ],
        axis=-1,
    )


def rotate_back(grad_rot, cosine, sine_tab, factor):
    half_dim = grad_rot.shape[-1] // 2
    first_half = grad_rot[..., :half_dim]
    second = grad_rot[..., half_dim:]
    cosine = cosine[:, None, :]
    sine_tab = sine_tab[:, None, :]
    factor = factor[:, None, :]
    return jnp.concatenate(
        [
            (first_half * cosine + second * sine_tab) * factor,
            (second * cosine - first_half * sine_tab) * factor,
        ],
        axis=-1,
    )


def plain_dot(first_op, second_op):
    return jnp.dot(first_op, second_op, preferred_element_type=jnp.float32)


def contract_last(first_op, second_op):
    return lax.dot_general(
        first_op, second_op, (((1,), (1,)), ((), ())), preferred_element_type=jnp.float32
    )


def contract_first(first_op, second_op):
    return lax.dot_general(
        first_op, second_op, (((0,), (0,)), ((), ())), preferred_element_type=jnp.float32
    )


class Ring:
    def __init__(self):
        self.devices = lax.axis_size("dp")
        self.chips = self.devices // 2
        half = self.chips // 2
        self.order = [2 * a for a in range(half)] + [2 * a + 1 for a in reversed(range(half))]
        self.index = lax.axis_index("dp")
        self.core = self.index % 2
        chip = self.index // 2
        self.place = jnp.where(chip % 2 == 0, chip // 2, self.chips - 1 - chip // 2)
        self.near = self.chips // 2
        self.far = self.chips - 1 - self.near

    def shift(self, rows, step):
        pairs = [
            (self.order[i] * 2 + c, self.order[(i + step) % self.chips] * 2 + c)
            for i in range(self.chips)
            for c in range(2)
        ]
        return lax.ppermute(rows, "dp", pairs)

    def swap(self, rows):
        return lax.ppermute(rows, "dp", [(i, i ^ 1) for i in range(self.devices)])

    def hops(self, flip):
        return (self.far, self.near) if flip else (self.near, self.far)

    def block_table(self):
        spot = (self.place + jnp.arange(self.chips, dtype=jnp.int32)) % self.chips
        chip = jnp.where(spot < self.chips // 2, 2 * spot, 2 * (self.chips - 1 - spot) + 1)
        return jnp.concatenate([chip * 2 + self.core, chip * 2 + 1 - self.core]).astype(jnp.int32)

    def gather(self, shard, flip):
        up, down = self.hops(flip)
        pieces = [None] * self.chips
        pieces[0] = shard
        moving_up, moving_down = shard, shard
        for step in range(1, max(up, down) + 1):
            if step <= up:
                moving_up = self.shift(moving_up, 1)
                pieces[self.chips - step] = moving_up
            if step <= down:
                moving_down = self.shift(moving_down, -1)
                pieces[step] = moving_down
        return pieces

    def reduce(self, term, flip):
        up, down = self.hops(flip)
        moving_up = term(up).astype(jnp.bfloat16)
        moving_down = term(self.chips - down).astype(jnp.bfloat16)
        for step in range(1, max(up, down) + 1):
            if step <= up:
                moving_up = self.shift(moving_up, 1)
                if step < up:
                    moving_up = (moving_up.astype(jnp.float32) + term(up - step)).astype(
                        jnp.bfloat16
                    )
            if step <= down:
                moving_down = self.shift(moving_down, -1)
                if step < down:
                    moving_down = (
                        moving_down.astype(jnp.float32) + term(self.chips - down + step)
                    ).astype(jnp.bfloat16)
        return term(0) + moving_up.astype(jnp.float32) + moving_down.astype(jnp.float32)

    def reduce_exact(self, parts, flip):
        up, down = self.hops(flip)
        moving_up, moving_down = parts(up), parts(self.chips - down)
        for step in range(1, max(up, down) + 1):
            if step <= up:
                moving_up = self.shift(moving_up, 1)
                if step < up:
                    moving_up = moving_up + parts(up - step)
            if step <= down:
                moving_down = self.shift(moving_down, -1)
                if step < down:
                    moving_down = moving_down + parts(self.chips - down + step)
        return parts(0) + moving_up + moving_down


def move_blocks(rows, table, outward):
    blocks = table.shape[0]
    width = rows.shape[1] // blocks

    def kernel(table_ref, in_ref, out_ref):
        for place in range(blocks):
            there = pl.ds(pl.multiple_of(table_ref[place] * width, width), width)
            here = pl.ds(place * width, width)
            if outward:
                out_ref[:, there] = in_ref[:, here]
            else:
                out_ref[:, here] = in_ref[:, there]

    if width % 128:
        order = table
        if outward:
            order = jnp.sum(
                jnp.where(table[None, :] == jnp.arange(blocks)[:, None], jnp.arange(blocks), 0),
                axis=1,
            )
        return jnp.take(rows.reshape(rows.shape[0], blocks, width), order, axis=1).reshape(
            rows.shape
        )
    return pl.pallas_call(
        kernel,
        out_shape=jax.ShapeDtypeStruct(rows.shape, rows.dtype),
        in_specs=[
            pl.BlockSpec(memory_space=pltpu.SMEM),
            pl.BlockSpec(memory_space=pltpu.VMEM),
        ],
        out_specs=pl.BlockSpec(memory_space=pltpu.VMEM),
    )(table, rows)


def swap_mp(rows):
    return lax.ppermute(rows, "mp", [(0, 1), (1, 0)])


def gather_rows(rows_low):
    return jnp.concatenate([rows_low, swap_mp(rows_low)], axis=0)


def scatter_rows(terms):
    half_rows = terms.shape[0] // 2
    arrived = swap_mp(terms[half_rows:].astype(jnp.bfloat16))
    return terms[:half_rows] + arrived.astype(jnp.float32)


def tie(value, other):
    return lax.optimization_barrier((value, other))[0]


def on_device(
    tokens_in,
    teacher,
    valid_mask,
    group_of,
    prompt_len,
    ln1_gain,
    ln1_bias,
    w_query,
    w_key,
    w_value,
    w_gate,
    w_out,
    ln2_gain,
    ln2_bias,
    w_up,
    w_down,
):
    half_rows = tokens_in.shape[0]
    model_dim = tokens_in.shape[1]
    seg_len = half_rows * lax.axis_size("mp")
    seg_count = group_of.shape[0]
    group_count = prompt_len.shape[0]
    heads_local = w_query.shape[1] // DK
    token_total = seg_len * seg_count
    dp_index = lax.axis_index("dp")
    mp_index = lax.axis_index("mp")
    ring = Ring()
    own_width = model_dim // 2
    table = ring.block_table()

    segment_ids = jnp.arange(seg_count, dtype=jnp.int32)
    my_group = jnp.sum(jnp.where(segment_ids == dp_index, group_of, 0))
    first_member = jnp.min(jnp.where(group_of == my_group, segment_ids, seg_count))
    prompt_flag = (first_member == dp_index).astype(jnp.float32)
    group_match = jnp.arange(group_count, dtype=jnp.int32) == my_group
    group_onehot = group_match.astype(jnp.float32)
    prompt_size = jnp.sum(jnp.where(group_match, prompt_len, 0))
    own_ids = mp_index * half_rows + jnp.arange(half_rows, dtype=jnp.int32)
    other_ids = (1 - mp_index) * half_rows + jnp.arange(half_rows, dtype=jnp.int32)
    token_ids = jnp.concatenate([own_ids, other_ids])
    loss_mask = valid_mask[0].astype(jnp.float32) * jnp.where(
        prompt_flag > 0, own_ids < prompt_size, True
    ).astype(jnp.float32)
    valid_count = lax.psum(jnp.sum(loss_mask.astype(jnp.int32)), ("dp", "mp")).astype(jnp.float32)

    vectors = jnp.stack([ln1_gain, ln1_bias, ln2_gain, ln2_bias])
    vector_own = jnp.concatenate(ring.gather(vectors, False), axis=1)
    vectors_full = jnp.concatenate([vector_own, ring.swap(vector_own)], axis=1).astype(jnp.float32)
    gain_one, bias_one, gain_two, bias_two = (vectors_full[i] for i in range(4))

    groups = [
        jnp.concatenate([w_key, w_value], axis=1),
        jnp.concatenate([w_query, w_gate], axis=1),
        w_out,
        w_up,
        w_down,
    ]
    gathered = []
    for i, shard in enumerate(groups):
        if i >= 2:
            shard = tie(shard, gathered[i - 2][0][ring.chips // 2])
        pieces = ring.gather(shard, i % 2 == 1)
        own = jnp.concatenate(pieces, axis=0)
        gathered.append((pieces, own, ring.swap(own)))
    full = [(own, other) for _, own, other in gathered]

    def times_full(rows, weight):
        return plain_dot(rows[:, :own_width], weight[0]) + plain_dot(rows[:, own_width:], weight[1])

    def times_full_t(rows, weight):
        return jnp.concatenate(
            [contract_last(rows, weight[0]), contract_last(rows, weight[1])], axis=1
        )

    key_width = w_key.shape[1]
    wkv, wqg, wo_full, wu_full, wd_full = full

    offset = jnp.where(prompt_flag > 0, 0, prompt_size)
    positions = (token_ids + offset).astype(jnp.float32)
    head_ids = (mp_index * heads_local + jnp.arange(heads_local, dtype=jnp.int32)).astype(
        jnp.float32
    )
    log_decay = jnp.log(1.0 - 2.0 ** (-5.0 - head_ids))
    before_end = token_ids < prompt_size
    state_age = (prompt_size - 1 - token_ids).astype(jnp.float32)
    state_weighting = jnp.where(
        (before_end & (prompt_flag > 0))[:, None],
        jnp.exp(log_decay[None, :] * jnp.maximum(state_age, 0.0)[:, None]),
        0.0,
    )
    float_ids = token_ids.astype(jnp.float32)
    continuation_factor = (1.0 - prompt_flag) * jnp.exp(
        log_decay[None, :] * (float_ids + 1.0)[:, None]
    )
    distance = float_ids[:, None] - float_ids[None, :]
    decay_mat = jnp.where(
        distance[None] >= 0.0,
        jnp.exp(log_decay[:, None, None] * jnp.maximum(distance, 0.0)[None]),
        0.0,
    )
    token_rows = move_blocks(tokens_in, table, False).astype(jnp.float32)
    teacher_rows = move_blocks(teacher, table, False).astype(jnp.float32)
    normed_one, inv_one = norm_stats(token_rows, EPSILON)
    a_all = gather_rows((normed_one * gain_one + bias_one).astype(jnp.bfloat16))
    key_value = times_full(a_all, wkv)
    keys_raw = key_value[:, :key_width].reshape(seg_len, heads_local, DK)
    reduced_values = (
        key_value[:, key_width:].astype(jnp.bfloat16).reshape(seg_len, heads_local, DV)
    )
    query_gate = times_full(a_all, wqg)
    queries = query_gate[:, :key_width].reshape(seg_len, heads_local, DK)
    gate_pre = query_gate[:, key_width:]
    cosine, sine_tab, grow_fac = xpos_tables(positions, 1.0)
    _, _, shrink = xpos_tables(positions, -1.0)
    q_scale = DK ** (-0.5)
    rotated_keys = rotate_pairs(keys_raw, cosine, sine_tab, shrink).astype(jnp.bfloat16)
    local_state = jnp.einsum(
        "jld,jla->lda",
        (rotated_keys.astype(jnp.float32) * state_weighting[:, :, None]).astype(jnp.bfloat16),
        reduced_values,
        preferred_element_type=jnp.float32,
    )
    slots = (group_onehot[:, None, None, None] * (prompt_flag * local_state)[None]).astype(
        jnp.bfloat16
    )
    summed = lax.psum(slots, "dp")
    state_lookup = jnp.sum(
        summed.astype(jnp.float32) * group_onehot[:, None, None, None], axis=0
    ).astype(jnp.bfloat16)
    rotated_queries = (rotate_pairs(queries, cosine, sine_tab, grow_fac) * q_scale).astype(
        jnp.bfloat16
    )
    scores = jnp.einsum(
        "thk,nhk->htn", rotated_queries, rotated_keys, preferred_element_type=jnp.float32
    )
    weights_low = (scores * decay_mat).astype(jnp.bfloat16)
    retained_output = jnp.einsum(
        "htn,nhv->thv", weights_low, reduced_values, preferred_element_type=jnp.float32
    )
    carried_forward = jnp.einsum(
        "ozi,ziw->ozw", rotated_queries, state_lookup, preferred_element_type=jnp.float32
    )
    retained_output = retained_output + continuation_factor[:, :, None] * carried_forward
    grouped, inv_group = norm_stats(retained_output, GROUP_EPSILON)
    gate_act = jax.nn.silu(gate_pre).reshape(seg_len, heads_local, DV)
    gated_out = (gate_act * grouped).reshape(seg_len, heads_local * DV).astype(jnp.bfloat16)
    attn_own = scatter_rows(times_full_t(gated_out, wo_full))
    hidden_res = token_rows + attn_own
    normed_two, inv_two = norm_stats(hidden_res, EPSILON)
    c_all = gather_rows((normed_two * gain_two + bias_two).astype(jnp.bfloat16))
    up_pre = times_full(c_all, wu_full)
    up_act = jax.nn.gelu(up_pre, approximate=False).astype(jnp.bfloat16)
    ffn_own = scatter_rows(times_full_t(up_act, wd_full))
    block_out = hidden_res + ffn_own
    error_rows = block_out - teacher_rows
    weighted = loss_mask[:, None] * error_rows
    squared = lax.psum(jnp.sum(weighted * error_rows), ("dp", "mp"))
    grad_out = token_total / valid_count * weighted
    loss_value = squared / (valid_count * model_dim)

    block = model_dim // ring.devices

    def weight_grad(feature_side, other_side, flip):
        mine = jnp.concatenate(
            [feature_side[:, :own_width], ring.swap(feature_side[:, own_width:])], axis=0
        )
        both = jnp.concatenate([other_side, ring.swap(other_side)], axis=0)

        def term(k):
            return contract_first(mine[:, k * block : (k + 1) * block], both)

        return ring.reduce(term, flip)

    grad_ffn_all = gather_rows(grad_out.astype(jnp.bfloat16))
    grad_wd = weight_grad(grad_ffn_all, up_act, False)
    grad_up_act = times_full(grad_ffn_all, wd_full)
    _, gelu_pull = jax.vjp(lambda inner: jax.nn.gelu(inner, approximate=False), up_pre)
    grad_up = gelu_pull(grad_up_act)[0].astype(jnp.bfloat16)
    grad_wu = weight_grad(c_all, grad_up, True)
    grad_c = scatter_rows(times_full_t(grad_up, wu_full))
    grad_gain2_part = jnp.sum(grad_c * normed_two, axis=0)
    grad_bias2_part = jnp.sum(grad_c, axis=0)
    grad_hidden = grad_out + norm_back(grad_c * gain_two, normed_two, inv_two)
    grad_attn_all = gather_rows(grad_hidden.astype(jnp.bfloat16))
    grad_wo = weight_grad(grad_attn_all, gated_out, False)
    grad_gated = times_full(grad_attn_all, wo_full).reshape(seg_len, heads_local, DV)
    _, silu_pull = jax.vjp(jax.nn.silu, gate_pre)
    grad_gate = silu_pull((grad_gated * grouped).reshape(seg_len, heads_local * DV))[0].astype(
        jnp.bfloat16
    )
    grad_wg = weight_grad(a_all, grad_gate, True)
    retained_gradient = norm_back(grad_gated * gate_act, grouped, inv_group).astype(jnp.bfloat16)
    state_grad_own = jnp.einsum(
        "ybn,ybw->bnw",
        (rotated_queries.astype(jnp.float32) * continuation_factor[:, :, None]).astype(
            jnp.bfloat16
        ),
        retained_gradient,
        preferred_element_type=jnp.float32,
    )
    grad_slots = (group_onehot[:, None, None, None] * state_grad_own[None]).astype(jnp.bfloat16)
    grad_summed = lax.psum(grad_slots, "dp")
    grad_weights = jnp.einsum(
        "thv,nhv->htn", retained_gradient, reduced_values, preferred_element_type=jnp.float32
    )
    grad_values = jnp.einsum(
        "htn,thv->nhv", weights_low, retained_gradient, preferred_element_type=jnp.float32
    )
    grad_scores = (grad_weights * decay_mat).astype(jnp.bfloat16)
    grad_q_rot = jnp.einsum(
        "htn,nhk->thk", grad_scores, rotated_keys, preferred_element_type=jnp.float32
    )
    grad_q_rot = grad_q_rot + continuation_factor[:, :, None] * jnp.einsum(
        "mjr,jwr->mjw", retained_gradient, state_lookup, preferred_element_type=jnp.float32
    )
    grad_k_rot = jnp.einsum(
        "htn,thk->nhk", grad_scores, rotated_queries, preferred_element_type=jnp.float32
    )
    grad_queries = (
        rotate_back(grad_q_rot * q_scale, cosine, sine_tab, grow_fac)
        .reshape(seg_len, heads_local * DK)
        .astype(jnp.bfloat16)
    )
    grad_wq = weight_grad(a_all, grad_queries, False)
    state_gradient = (
        prompt_flag
        * jnp.sum(grad_summed.astype(jnp.float32) * group_onehot[:, None, None, None], axis=0)
    ).astype(jnp.bfloat16)
    grad_k_rot = grad_k_rot + state_weighting[:, :, None] * jnp.einsum(
        "ilm,lpm->ilp", reduced_values, state_gradient, preferred_element_type=jnp.float32
    )
    grad_values = grad_values + state_weighting[:, :, None] * jnp.einsum(
        "zdo,doi->zdi", rotated_keys, state_gradient, preferred_element_type=jnp.float32
    )
    grad_keys = (
        rotate_back(grad_k_rot, cosine, sine_tab, shrink)
        .reshape(seg_len, heads_local * DK)
        .astype(jnp.bfloat16)
    )
    grad_vlow = grad_values.reshape(seg_len, heads_local * DV).astype(jnp.bfloat16)
    grad_key_value = jnp.concatenate([grad_keys, grad_vlow], axis=1)
    grad_wkv = weight_grad(a_all, grad_key_value, True)
    grad_query_gate = jnp.concatenate([grad_queries, grad_gate], axis=1)
    grad_a = scatter_rows(
        times_full_t(grad_query_gate, wqg) + times_full_t(grad_key_value, wkv)
    )
    grad_gain1_part = jnp.sum(grad_a * normed_one, axis=0)
    grad_bias1_part = jnp.sum(grad_a, axis=0)
    grad_tokens = grad_hidden + norm_back(grad_a * gain_one, normed_one, inv_one)

    sums = jnp.stack([grad_gain1_part, grad_bias1_part, grad_gain2_part, grad_bias2_part])
    sums = sums + swap_mp(sums)
    sums = sums[:, :own_width] + ring.swap(sums[:, own_width:])
    sums = ring.reduce_exact(lambda k: sums[:, k * block : (k + 1) * block], False)

    return (
        move_blocks(block_out, table, True),
        move_blocks(grad_tokens, table, True),
        loss_value,
        sums[0],
        sums[1],
        grad_wq,
        grad_wkv[:, :key_width],
        grad_wkv[:, key_width:],
        grad_wg,
        grad_wo,
        sums[2],
        sums[3],
        grad_wu,
        grad_wd,
    )


def solution(mesh):
    return jax.shard_map(
        on_device,
        mesh=mesh,
        in_specs=(
            P(("dp", "mp"), None),
            P(("dp", "mp"), None),
            P("dp", "mp"),
            P(),
            P(),
            P("dp"),
            P("dp"),
            P("dp", "mp"),
            P("dp", "mp"),
            P("dp", "mp"),
            P("dp", "mp"),
            P("dp", "mp"),
            P("dp"),
            P("dp"),
            P("dp", "mp"),
            P("dp", "mp"),
        ),
        out_specs=(
            P(("dp", "mp"), None),
            P(("dp", "mp"), None),
            P(),
            P("dp"),
            P("dp"),
            P("dp", "mp"),
            P("dp", "mp"),
            P("dp", "mp"),
            P("dp", "mp"),
            P("dp", "mp"),
            P("dp"),
            P("dp"),
            P("dp", "mp"),
            P("dp", "mp"),
        ),
        check_vma=False,
    )
```

```python
import math

import jax
import jax.numpy as jnp
from jax import lax
from jax.experimental import pallas as pl
from jax.experimental.pallas import tpu as pltpu
from jax.sharding import PartitionSpec as P

DK = 256
DV = 512


EPSILON = 1e-05
GROUP_EPSILON = 0.05


def norm_stats(values, floor_eps):
    center = jnp.mean(values, axis=-1, keepdims=True)
    shifted = values - center
    inv_std = lax.rsqrt(jnp.mean(shifted * shifted, axis=-1, keepdims=True) + floor_eps)
    return (shifted * inv_std, inv_std)


def norm_back(grad_in, normed, inv_std):
    mean_grad = jnp.mean(grad_in, axis=-1, keepdims=True)
    mean_proj = jnp.mean(grad_in * normed, axis=-1, keepdims=True)
    return (grad_in - mean_grad - normed * mean_proj) * inv_std


def xpos_tables(positions, direction):
    half_dim = DK // 2
    pair_index = jnp.arange(half_dim, dtype=jnp.float32)
    frequency = jnp.exp(-(2.0 * pair_index / DK) * math.log(10000.0))
    base_ratio = (2.0 * pair_index / DK + 0.4) / 1.4
    angles = positions[:, None] * frequency[None, :]
    factor = jnp.exp(direction * (positions[:, None] / 512.0) * jnp.log(base_ratio)[None, :])
    return (jnp.cos(angles), jnp.sin(angles), factor)


def rotate_pairs(values, cosine, sine_tab, factor):
    half_dim = values.shape[-1] // 2
    first_half = values[..., :half_dim]
    second = values[..., half_dim:]
    cosine = cosine[:, None, :]
    sine_tab = sine_tab[:, None, :]
    factor = factor[:, None, :]
    return jnp.concatenate(
        [
            (first_half * cosine - second * sine_tab) * factor,
            (second * cosine + first_half * sine_tab) * factor,
        ],
        axis=-1,
    )


def rotate_back(grad_rot, cosine, sine_tab, factor):
    half_dim = grad_rot.shape[-1] // 2
    first_half = grad_rot[..., :half_dim]
    second = grad_rot[..., half_dim:]
    cosine = cosine[:, None, :]
    sine_tab = sine_tab[:, None, :]
    factor = factor[:, None, :]
    return jnp.concatenate(
        [
            (first_half * cosine + second * sine_tab) * factor,
            (second * cosine - first_half * sine_tab) * factor,
        ],
        axis=-1,
    )


def plain_dot(first_op, second_op):
    return jnp.dot(first_op, second_op, preferred_element_type=jnp.float32)


def contract_last(first_op, second_op):
    return lax.dot_general(
        first_op, second_op, (((1,), (1,)), ((), ())), preferred_element_type=jnp.float32
    )


def contract_first(first_op, second_op):
    return lax.dot_general(
        first_op, second_op, (((0,), (0,)), ((), ())), preferred_element_type=jnp.float32
    )


class Ring:
    def __init__(self):
        self.devices = lax.axis_size("dp")
        self.chips = self.devices // 2
        half = self.chips // 2
        self.order = [2 * a for a in range(half)] + [2 * a + 1 for a in reversed(range(half))]
        self.index = lax.axis_index("dp")
        self.core = self.index % 2
        chip = self.index // 2
        self.place = jnp.where(chip % 2 == 0, chip // 2, self.chips - 1 - chip // 2)
        self.near = self.chips // 2
        self.far = self.chips - 1 - self.near

    def shift(self, rows, step):
        pairs = [
            (self.order[i] * 2 + c, self.order[(i + step) % self.chips] * 2 + c)
            for i in range(self.chips)
            for c in range(2)
        ]
        return lax.ppermute(rows, "dp", pairs)

    def swap(self, rows):
        return lax.ppermute(rows, "dp", [(i, i ^ 1) for i in range(self.devices)])

    def hops(self, flip):
        return (self.far, self.near) if flip else (self.near, self.far)

    def block_table(self):
        spot = (self.place + jnp.arange(self.chips, dtype=jnp.int32)) % self.chips
        chip = jnp.where(spot < self.chips // 2, 2 * spot, 2 * (self.chips - 1 - spot) + 1)
        return jnp.concatenate([chip * 2 + self.core, chip * 2 + 1 - self.core]).astype(jnp.int32)


class RingSum:
    def __init__(self, ring, full, flip):
        self.ring = ring
        self.full = full
        self.block = full.shape[0] // ring.chips
        self.up, self.down = ring.hops(flip)
        self.moving = [self.term(self.up), self.term(ring.chips - self.down)]
        self.count = 0

    def term(self, k):
        return self.full[k * self.block : (k + 1) * self.block]

    def step(self):
        ring = self.ring
        self.count += 1
        for way, hops, k in (
            (0, self.up, self.up - self.count),
            (1, self.down, ring.chips - self.down + self.count),
        ):
            if self.count <= hops:
                moved = ring.shift(self.moving[way], 1 - 2 * way)
                if self.count < hops:
                    moved = moved.astype(jnp.float32) + self.term(k).astype(jnp.float32)
                    moved = moved.astype(jnp.bfloat16)
                self.moving[way] = moved

    def run(self, steps):
        for _ in range(min(steps, max(self.up, self.down) - self.count)):
            self.step()

    def result(self):
        self.run(self.ring.chips)
        return (
            self.term(0).astype(jnp.float32)
            + self.moving[0].astype(jnp.float32)
            + self.moving[1].astype(jnp.float32)
        )


def gather_ring(shards, call_id=1):
    devices = lax.axis_size("dp")
    chips = devices // 2
    half = chips // 2
    rows = shards[0].shape[0]
    count = len(shards)
    parts = 2
    piece = rows // parts
    hops = ((half, half - 1), (half - 1, half))

    def kernel(*refs):
        ins, outs = refs[:count], refs[count : 2 * count]
        own_sem, side_send, side_recv, ring_send, ring_recv = refs[2 * count :]
        index = lax.axis_index("dp")
        core, chip = index % 2, index // 2
        odd = chip % 2
        place = (1 - odd) * (chip // 2) + odd * (chips - 1 - chip // 2)

        def device_at(spot, which):
            spot = (spot + 2 * chips) % chips
            upper = spot // half
            there = (1 - upper) * (2 * spot) + upper * (2 * (chips - 1 - spot) + 1)
            return there * 2 + which

        def window(spot, which, part):
            first = device_at(spot, which) * rows + part * piece
            return pl.ds(pl.multiple_of(first, piece), piece)

        partner = chip * 2 + 1 - core
        neighbours = (device_at(place + 1, core), device_at(place - 1, core))

        barrier = pltpu.get_barrier_semaphore()
        for target in (*neighbours, partner):
            pl.semaphore_signal(
                barrier, inc=1, device_id={"dp": target}, device_id_type=pl.DeviceIdType.MESH
            )
        pl.semaphore_wait(barrier, 3)

        sends = []

        def source(j, spot, part, own):
            if own:
                return ins[j].at[pl.ds(part * piece, piece)]
            return outs[j].at[window(spot, core, part)]

        def ring_copy(j, way, part, hop):
            spot = place - (hop - 1) * (1 - 2 * way)
            return pltpu.make_async_remote_copy(
                src_ref=source(j, spot, part, hop == 1),
                dst_ref=outs[j].at[window(spot, core, part)],
                send_sem=ring_send.at[j, way, part, hop - 1],
                recv_sem=ring_recv.at[j, way, part, hop - 1],
                device_id={"dp": neighbours[way]},
                device_id_type=pl.DeviceIdType.MESH,
            )

        def ring_arrival(j, way, part, hop):
            spot = place - hop * (1 - 2 * way)
            here = outs[j].at[window(spot, core, part)]
            return pltpu.make_async_remote_copy(
                src_ref=here,
                dst_ref=here,
                send_sem=ring_send.at[j, way, part, hop - 1],
                recv_sem=ring_recv.at[j, way, part, hop - 1],
                device_id={"dp": neighbours[way]},
                device_id_type=pl.DeviceIdType.MESH,
            )

        def side_copy(j, part, slot, spot, own):
            return pltpu.make_async_remote_copy(
                src_ref=source(j, spot, part, own),
                dst_ref=outs[j].at[window(spot, core, part)],
                send_sem=side_send.at[j, part, slot],
                recv_sem=side_recv.at[j, part, slot],
                device_id={"dp": partner},
                device_id_type=pl.DeviceIdType.MESH,
            )

        def side_arrival(j, part, slot, spot):
            here = outs[j].at[window(spot, 1 - core, part)]
            return pltpu.make_async_remote_copy(
                src_ref=here,
                dst_ref=here,
                send_sem=side_send.at[j, part, slot],
                recv_sem=side_recv.at[j, part, slot],
                device_id={"dp": partner},
                device_id_type=pl.DeviceIdType.MESH,
            )

        def launch(copy):
            copy.start()
            sends.append(copy)

        for part in range(parts):
            for j in range(count):
                for way in range(2):
                    launch(ring_copy(j, way, part, 1))
        owns = []
        for part in range(parts):
            for j in range(count):
                launch(side_copy(j, part, 0, place, True))
                own = pltpu.make_async_copy(
                    source(j, place, part, True),
                    outs[j].at[window(place, core, part)],
                    own_sem.at[j, part],
                )
                own.start()
                owns.append(own)
        for hop in range(1, half + 1):
            for part in range(parts):
                for j in range(count):
                    for way in range(2):
                        if hop <= hops[way][part]:
                            ring_arrival(j, way, part, hop).wait_recv()
                            if hop < hops[way][part]:
                                launch(ring_copy(j, way, part, hop + 1))
                            turn = 1 - 2 * way
                            slot = (chips - hop * turn) % chips
                            launch(side_copy(j, part, slot, place - hop * turn, False))
        for own in owns:
            own.wait()
        for copy in sends:
            copy.wait_send()
        for slot in range(chips):
            for part in range(parts):
                for j in range(count):
                    side_arrival(j, part, slot, place + slot).wait_recv()

    total = sum(shard.shape[1] for shard in shards) * rows * 2
    return pl.pallas_call(
        kernel,
        out_shape=[
            jax.ShapeDtypeStruct((devices * rows, shard.shape[1]), shard.dtype) for shard in shards
        ],
        in_specs=[pl.BlockSpec(memory_space=pl.ANY)] * count,
        out_specs=[pl.BlockSpec(memory_space=pl.ANY)] * count,
        scratch_shapes=[
            pltpu.SemaphoreType.DMA((count, parts)),
            pltpu.SemaphoreType.DMA((count, parts, chips)),
            pltpu.SemaphoreType.DMA((count, parts, chips)),
            pltpu.SemaphoreType.DMA((count, 2, parts, half)),
            pltpu.SemaphoreType.DMA((count, 2, parts, half)),
        ],
        compiler_params=pltpu.CompilerParams(collective_id=call_id, has_side_effects=True),
        cost_estimate=pl.CostEstimate(
            flops=0, bytes_accessed=total * devices * 4, transcendentals=0
        ),
    )(*shards)


def exchange_blocks(blocks):
    dp_size, mp_size = lax.axis_size("dp"), lax.axis_size("mp")
    total = dp_size * mp_size

    def kernel(in_ref, out_ref, send_sem, recv_sem):
        dp_index = lax.axis_index("dp")
        me = dp_index * mp_size + lax.axis_index("mp")

        def place(offset):
            target = (me + offset) % total
            return target // mp_size, target % mp_size

        barrier = pltpu.get_barrier_semaphore()

        def greet(offset, carry):
            row, col = place(offset)
            pl.semaphore_signal(
                barrier, inc=1, device_id=(row, col), device_id_type=pl.DeviceIdType.MESH
            )
            return carry

        lax.fori_loop(1, total, greet, 0)
        pl.semaphore_wait(barrier, total - 1)

        def send(offset):
            row, col = place(offset)
            return pltpu.make_async_remote_copy(
                src_ref=in_ref.at[row],
                dst_ref=out_ref.at[me],
                send_sem=send_sem.at[offset],
                recv_sem=recv_sem.at[offset],
                device_id=(row, col),
                device_id_type=pl.DeviceIdType.MESH,
            )

        def begin(offset, carry):
            send(offset).start()
            return carry

        lax.fori_loop(1, total, begin, 0)
        out_ref[me] = in_ref[dp_index]

        def finish(offset, carry):
            sender = (me + total - offset) % total
            send(offset).wait_send()
            pltpu.make_async_remote_copy(
                src_ref=out_ref.at[sender],
                dst_ref=out_ref.at[sender],
                send_sem=send_sem.at[offset],
                recv_sem=recv_sem.at[offset],
                device_id=place(offset),
                device_id_type=pl.DeviceIdType.MESH,
            ).wait_recv()
            return carry

        lax.fori_loop(1, total, finish, 0)

    return pl.pallas_call(
        kernel,
        out_shape=jax.ShapeDtypeStruct((total, *blocks.shape[1:]), blocks.dtype),
        in_specs=[pl.BlockSpec(memory_space=pltpu.VMEM)],
        out_specs=pl.BlockSpec(memory_space=pltpu.VMEM),
        scratch_shapes=[
            pltpu.SemaphoreType.DMA((total,)),
            pltpu.SemaphoreType.DMA((total,)),
        ],
        compiler_params=pltpu.CompilerParams(collective_id=2, has_side_effects=True),
    )(blocks)


def move_blocks(rows, table, outward):
    blocks = table.shape[0]
    width = rows.shape[1] // blocks

    def kernel(table_ref, in_ref, out_ref):
        for place in range(blocks):
            there = pl.ds(pl.multiple_of(table_ref[place] * width, width), width)
            here = pl.ds(place * width, width)
            if outward:
                out_ref[:, there] = in_ref[:, here]
            else:
                out_ref[:, here] = in_ref[:, there]

    if width % 128:
        order = table
        if outward:
            order = jnp.sum(
                jnp.where(table[None, :] == jnp.arange(blocks)[:, None], jnp.arange(blocks), 0),
                axis=1,
            )
        return jnp.take(rows.reshape(rows.shape[0], blocks, width), order, axis=1).reshape(
            rows.shape
        )
    return pl.pallas_call(
        kernel,
        out_shape=jax.ShapeDtypeStruct(rows.shape, rows.dtype),
        in_specs=[
            pl.BlockSpec(memory_space=pltpu.SMEM),
            pl.BlockSpec(memory_space=pltpu.VMEM),
        ],
        out_specs=pl.BlockSpec(memory_space=pltpu.VMEM),
    )(table, rows)


def swap_mp(rows):
    return lax.ppermute(rows, "mp", [(0, 1), (1, 0)])


def gather_rows(rows_low):
    return jnp.concatenate([rows_low, swap_mp(rows_low)], axis=0)


def scatter_rows(terms):
    half_rows = terms.shape[0] // 2
    arrived = swap_mp(terms[half_rows:].astype(jnp.bfloat16))
    return terms[:half_rows] + arrived.astype(jnp.float32)


def tie(value, other):
    return lax.optimization_barrier((value, other))[0]


def on_device(
    tokens_in,
    teacher,
    valid_mask,
    group_of,
    prompt_len,
    ln1_gain,
    ln1_bias,
    w_query,
    w_key,
    w_value,
    w_gate,
    w_out,
    ln2_gain,
    ln2_bias,
    w_up,
    w_down,
):
    half_rows = tokens_in.shape[0]
    model_dim = tokens_in.shape[1]
    seg_len = half_rows * lax.axis_size("mp")
    seg_count = group_of.shape[0]
    group_count = prompt_len.shape[0]
    heads_local = w_query.shape[1] // DK
    token_total = seg_len * seg_count
    dp_index = lax.axis_index("dp")
    mp_index = lax.axis_index("mp")
    ring = Ring()
    own_width = model_dim // 2
    table = ring.block_table()

    segment_ids = jnp.arange(seg_count, dtype=jnp.int32)
    my_group = jnp.sum(jnp.where(segment_ids == dp_index, group_of, 0))
    first_member = jnp.min(jnp.where(group_of == my_group, segment_ids, seg_count))
    prompt_flag = (first_member == dp_index).astype(jnp.float32)
    group_match = jnp.arange(group_count, dtype=jnp.int32) == my_group
    group_onehot = group_match.astype(jnp.float32)
    prompt_size = jnp.sum(jnp.where(group_match, prompt_len, 0))
    own_ids = mp_index * half_rows + jnp.arange(half_rows, dtype=jnp.int32)
    other_ids = (1 - mp_index) * half_rows + jnp.arange(half_rows, dtype=jnp.int32)
    token_ids = jnp.concatenate([own_ids, other_ids])
    loss_mask = valid_mask[0].astype(jnp.float32) * jnp.where(
        prompt_flag > 0, own_ids < prompt_size, True
    ).astype(jnp.float32)
    block = model_dim // ring.devices

    def packed(rows, scalar):
        split = rows.reshape(rows.shape[0], -1, block).transpose(1, 0, 2)
        split = jnp.pad(split, ((0, 0), (0, 0), (0, 128 - block)))
        extra = jnp.broadcast_to(scalar, (split.shape[0], 8 - rows.shape[0], 128))
        return jnp.concatenate([split, extra], axis=1)

    vectors = jnp.stack([ln1_gain, ln1_bias, ln2_gain, ln2_bias]).astype(jnp.float32)
    from_all = exchange_blocks(
        packed(jnp.tile(vectors, (1, ring.devices)), jnp.sum(loss_mask))
    )
    valid_count = jnp.sum(from_all[:, 4, 0])
    by_row = from_all.reshape(ring.devices, -1, 8, 128)[:, 0, :4, :block]
    gain_one, bias_one, gain_two, bias_two = (
        by_row[:, i].reshape(1, model_dim) for i in range(4)
    )

    def gather_all(shard):
        return lax.all_gather(shard, "dp", axis=0, tiled=True)

    offset = jnp.where(prompt_flag > 0, 0, prompt_size)
    positions = (token_ids + offset).astype(jnp.float32)
    head_ids = (mp_index * heads_local + jnp.arange(heads_local, dtype=jnp.int32)).astype(
        jnp.float32
    )
    log_decay = jnp.log(1.0 - 2.0 ** (-5.0 - head_ids))
    before_end = token_ids < prompt_size
    state_age = (prompt_size - 1 - token_ids).astype(jnp.float32)
    state_weighting = jnp.where(
        (before_end & (prompt_flag > 0))[:, None],
        jnp.exp(log_decay[None, :] * jnp.maximum(state_age, 0.0)[:, None]),
        0.0,
    )
    float_ids = token_ids.astype(jnp.float32)
    continuation_factor = (1.0 - prompt_flag) * jnp.exp(
        log_decay[None, :] * (float_ids + 1.0)[:, None]
    )
    distance = float_ids[:, None] - float_ids[None, :]
    decay_mat = jnp.where(
        distance[None] >= 0.0,
        jnp.exp(log_decay[:, None, None] * jnp.maximum(distance, 0.0)[None]),
        0.0,
    )
    token_rows = tokens_in.astype(jnp.float32)
    teacher_rows = teacher.astype(jnp.float32)
    normed_one, inv_one = norm_stats(token_rows, EPSILON)
    a_own = (normed_one * gain_one + bias_one).astype(jnp.bfloat16)
    a_all = gather_rows(a_own)
    wk_full, wv_full = gather_ring([tie(w_key, a_own), w_value])
    keys_raw = plain_dot(a_all, wk_full).reshape(seg_len, heads_local, DK)
    reduced_values = (
        plain_dot(a_all, wv_full).astype(jnp.bfloat16).reshape(seg_len, heads_local, DV)
    )
    cosine, sine_tab, grow_fac = xpos_tables(positions, 1.0)
    _, _, shrink = xpos_tables(positions, -1.0)
    q_scale = DK ** (-0.5)
    rotated_keys = rotate_pairs(keys_raw, cosine, sine_tab, shrink).astype(jnp.bfloat16)
    local_state = jnp.einsum(
        "jld,jla->lda",
        (rotated_keys.astype(jnp.float32) * state_weighting[:, :, None]).astype(jnp.bfloat16),
        reduced_values,
        preferred_element_type=jnp.float32,
    )
    slots = (group_onehot[:, None, None, None] * (prompt_flag * local_state)[None]).astype(
        jnp.bfloat16
    )
    summed = lax.psum(slots, "dp")
    wq_full, wg_full = gather_ring([tie(w_query, slots), w_gate])
    both_ffn = gather_all(jnp.concatenate([w_up, tie(w_down, wq_full[:8])], axis=1))
    wu_full, wd_full = both_ffn[:, : w_up.shape[1]], both_ffn[:, w_up.shape[1] :]
    (wo_full,) = gather_ring([tie(w_out, wq_full[:8])], 3)
    state_lookup = jnp.sum(
        summed.astype(jnp.float32) * group_onehot[:, None, None, None], axis=0
    ).astype(jnp.bfloat16)
    queries = plain_dot(a_all, wq_full).reshape(seg_len, heads_local, DK)
    gate_pre = plain_dot(a_all, wg_full)
    rotated_queries = (rotate_pairs(queries, cosine, sine_tab, grow_fac) * q_scale).astype(
        jnp.bfloat16
    )
    scores = jnp.einsum(
        "thk,nhk->htn", rotated_queries, rotated_keys, preferred_element_type=jnp.float32
    )
    weights_low = (scores * decay_mat).astype(jnp.bfloat16)
    retained_output = jnp.einsum(
        "htn,nhv->thv", weights_low, reduced_values, preferred_element_type=jnp.float32
    )
    carried_forward = jnp.einsum(
        "ozi,ziw->ozw", rotated_queries, state_lookup, preferred_element_type=jnp.float32
    )
    retained_output = retained_output + continuation_factor[:, :, None] * carried_forward
    grouped, inv_group = norm_stats(retained_output, GROUP_EPSILON)
    gate_act = jax.nn.silu(gate_pre).reshape(seg_len, heads_local, DV)
    gated_out = (gate_act * grouped).reshape(seg_len, heads_local * DV).astype(jnp.bfloat16)
    attn_own = scatter_rows(contract_last(gated_out, wo_full))
    hidden_res = token_rows + attn_own
    normed_two, inv_two = norm_stats(hidden_res, EPSILON)
    c_all = gather_rows((normed_two * gain_two + bias_two).astype(jnp.bfloat16))
    up_pre = plain_dot(c_all, wu_full)
    up_act = jax.nn.gelu(up_pre, approximate=False).astype(jnp.bfloat16)
    ffn_own = scatter_rows(contract_last(up_act, wd_full))
    block_out = hidden_res + ffn_own
    error_rows = block_out - teacher_rows
    weighted = loss_mask[:, None] * error_rows
    squared_own = jnp.sum(weighted * error_rows)
    grad_out = token_total / valid_count * weighted

    def weight_grad(feature_side, other_side, flip):
        mine = jnp.concatenate(
            [feature_side[:, :own_width], ring.swap(feature_side[:, own_width:])], axis=0
        )
        both = jnp.concatenate([other_side, ring.swap(other_side)], axis=0)
        return RingSum(ring, contract_first(mine, both).astype(jnp.bfloat16), flip)

    def in_order(rows):
        return move_blocks(rows, table, False)

    def then(value, *ring_sums):
        return tie(value, tuple(r.moving[way] for r in ring_sums for way in range(2)))

    grad_ffn_all = gather_rows(grad_out.astype(jnp.bfloat16))
    sum_wd = weight_grad(in_order(grad_ffn_all), up_act, False)
    grad_up_act = plain_dot(tie(grad_ffn_all, sum_wd.full[:16, :128]), wd_full)
    _, gelu_pull = jax.vjp(lambda inner: jax.nn.gelu(inner, approximate=False), up_pre)
    grad_up = gelu_pull(grad_up_act)[0].astype(jnp.bfloat16)
    sum_wu = weight_grad(in_order(c_all), grad_up, True)
    sum_wd.run(1)
    grad_up = tie(then(grad_up, sum_wd), sum_wu.full[:16, :128])
    grad_c_parts = contract_last(grad_up, wu_full)
    grad_c = scatter_rows(grad_c_parts)
    sum_wd.run(1)
    grad_c = then(grad_c, sum_wd)
    grad_gain2_part = jnp.sum(grad_c * normed_two, axis=0)
    grad_bias2_part = jnp.sum(grad_c, axis=0)
    grad_hidden = grad_out + norm_back(grad_c * gain_two, normed_two, inv_two)
    grad_attn_all = gather_rows(grad_hidden.astype(jnp.bfloat16))
    sum_wd.run(2)
    sum_wu.run(1)
    grad_attn_all = then(grad_attn_all, sum_wd, sum_wu)
    sum_wo = weight_grad(in_order(grad_attn_all), gated_out, False)
    grad_attn_all = tie(grad_attn_all, sum_wo.full[:16, :128])
    grad_gated = plain_dot(grad_attn_all, wo_full).reshape(seg_len, heads_local, DV)
    _, silu_pull = jax.vjp(jax.nn.silu, gate_pre)
    grad_gate = silu_pull((grad_gated * grouped).reshape(seg_len, heads_local * DV))[0].astype(
        jnp.bfloat16
    )
    retained_gradient = norm_back(grad_gated * gate_act, grouped, inv_group).astype(jnp.bfloat16)
    state_grad_own = jnp.einsum(
        "ybn,ybw->bnw",
        (rotated_queries.astype(jnp.float32) * continuation_factor[:, :, None]).astype(
            jnp.bfloat16
        ),
        retained_gradient,
        preferred_element_type=jnp.float32,
    )
    grad_slots = (group_onehot[:, None, None, None] * state_grad_own[None]).astype(jnp.bfloat16)
    grad_summed = lax.psum(grad_slots, "dp")
    sum_wu.run(2)
    a_order = in_order(a_all)
    grad_gate = tie(then(grad_gate, sum_wu), grad_slots[:, :, :8, :128])
    sum_wg = weight_grad(a_order, grad_gate, True)
    retained_gradient = tie(retained_gradient, sum_wg.full[:16, :128])
    sum_wu.run(1)
    sum_wo.run(1)
    grad_weights = jnp.einsum(
        "thv,nhv->htn", retained_gradient, reduced_values, preferred_element_type=jnp.float32
    )
    grad_values = jnp.einsum(
        "htn,thv->nhv", weights_low, retained_gradient, preferred_element_type=jnp.float32
    )
    grad_scores = then((grad_weights * decay_mat).astype(jnp.bfloat16), sum_wu, sum_wo)
    sum_wo.run(1)
    grad_q_rot = jnp.einsum(
        "htn,nhk->thk", grad_scores, rotated_keys, preferred_element_type=jnp.float32
    )
    grad_q_rot = grad_q_rot + continuation_factor[:, :, None] * jnp.einsum(
        "mjr,jwr->mjw", retained_gradient, state_lookup, preferred_element_type=jnp.float32
    )
    grad_k_rot = jnp.einsum(
        "htn,thk->nhk", grad_scores, rotated_queries, preferred_element_type=jnp.float32
    )
    grad_queries = (
        rotate_back(grad_q_rot * q_scale, cosine, sine_tab, grow_fac)
        .reshape(seg_len, heads_local * DK)
        .astype(jnp.bfloat16)
    )
    grad_queries = then(grad_queries, sum_wo)
    sum_wq = weight_grad(a_order, grad_queries, False)
    sum_wo.run(2)
    sum_wg.run(2)
    grad_summed = tie(then(grad_summed, sum_wo, sum_wg), sum_wq.full[:16, :128])
    state_gradient = (
        prompt_flag
        * jnp.sum(grad_summed.astype(jnp.float32) * group_onehot[:, None, None, None], axis=0)
    ).astype(jnp.bfloat16)
    grad_k_rot = grad_k_rot + state_weighting[:, :, None] * jnp.einsum(
        "ilm,lpm->ilp", reduced_values, state_gradient, preferred_element_type=jnp.float32
    )
    grad_values = grad_values + state_weighting[:, :, None] * jnp.einsum(
        "zdo,doi->zdi", rotated_keys, state_gradient, preferred_element_type=jnp.float32
    )
    grad_keys = (
        rotate_back(grad_k_rot, cosine, sine_tab, shrink)
        .reshape(seg_len, heads_local * DK)
        .astype(jnp.bfloat16)
    )
    grad_vlow = grad_values.reshape(seg_len, heads_local * DV).astype(jnp.bfloat16)
    grad_key_value = jnp.concatenate([grad_keys, grad_vlow], axis=1)
    sum_wg.run(1)
    grad_key_value = then(grad_key_value, sum_wg)
    sum_wkv = weight_grad(a_order, grad_key_value, True)
    grad_queries, grad_keys = (tie(x, sum_wkv.full[:16, :128]) for x in (grad_queries, grad_keys))
    grad_a = scatter_rows(
        contract_last(grad_queries, wq_full)
        + contract_last(grad_gate, wg_full)
        + contract_last(grad_keys, wk_full)
        + contract_last(grad_vlow, wv_full)
    )
    sum_wg.run(1)
    sum_wq.run(2)
    sum_wkv.run(1)
    grad_a = then(grad_a, sum_wg, sum_wq, sum_wkv)
    grad_gain1_part = jnp.sum(grad_a * normed_one, axis=0)
    grad_bias1_part = jnp.sum(grad_a, axis=0)
    grad_tokens = grad_hidden + norm_back(grad_a * gain_one, normed_one, inv_one)

    sums = jnp.stack([grad_gain1_part, grad_bias1_part, grad_gain2_part, grad_bias2_part])
    totals = jnp.sum(exchange_blocks(packed(sums, squared_own)), axis=0)
    loss_value = totals[4, 0] / (valid_count * model_dim)
    key_width = w_key.shape[1]
    grad_wkv = sum_wkv.result()

    return (
        block_out,
        grad_tokens,
        loss_value,
        totals[0, :block],
        totals[1, :block],
        sum_wq.result(),
        grad_wkv[:, :key_width],
        grad_wkv[:, key_width:],
        sum_wg.result(),
        sum_wo.result(),
        totals[2, :block],
        totals[3, :block],
        sum_wu.result(),
        sum_wd.result(),
    )


def solution(mesh):
    return jax.shard_map(
        on_device,
        mesh=mesh,
        in_specs=(
            P(("dp", "mp"), None),
            P(("dp", "mp"), None),
            P("dp", "mp"),
            P(),
            P(),
            P("dp"),
            P("dp"),
            P("dp", "mp"),
            P("dp", "mp"),
            P("dp", "mp"),
            P("dp", "mp"),
            P("dp", "mp"),
            P("dp"),
            P("dp"),
            P("dp", "mp"),
            P("dp", "mp"),
        ),
        out_specs=(
            P(("dp", "mp"), None),
            P(("dp", "mp"), None),
            P(),
            P("dp"),
            P("dp"),
            P("dp", "mp"),
            P("dp", "mp"),
            P("dp", "mp"),
            P("dp", "mp"),
            P("dp", "mp"),
            P("dp"),
            P("dp"),
            P("dp", "mp"),
            P("dp", "mp"),
        ),
        check_vma=False,
    )
```

```python
import functools
import math

import jax
import jax.numpy as jnp
from jax import lax
from jax.experimental import pallas as pl
from jax.experimental.pallas import tpu as pltpu
from jax.sharding import PartitionSpec as P

DK = 256
DV = 512


EPSILON = 1e-05
GROUP_EPSILON = 0.05


def norm_stats(values, floor_eps):
    center = jnp.mean(values, axis=-1, keepdims=True)
    shifted = values - center
    inv_std = lax.rsqrt(jnp.mean(shifted * shifted, axis=-1, keepdims=True) + floor_eps)
    return (shifted * inv_std, inv_std)


def norm_back(grad_in, normed, inv_std):
    mean_grad = jnp.mean(grad_in, axis=-1, keepdims=True)
    mean_proj = jnp.mean(grad_in * normed, axis=-1, keepdims=True)
    return (grad_in - mean_grad - normed * mean_proj) * inv_std


def xpos_tables(positions, direction):
    half_dim = DK // 2
    pair_index = jnp.arange(half_dim, dtype=jnp.float32)
    frequency = jnp.exp(-(2.0 * pair_index / DK) * math.log(10000.0))
    base_ratio = (2.0 * pair_index / DK + 0.4) / 1.4
    angles = positions[:, None] * frequency[None, :]
    factor = jnp.exp(direction * (positions[:, None] / 512.0) * jnp.log(base_ratio)[None, :])
    return (jnp.cos(angles), jnp.sin(angles), factor)


def rotate_pairs(values, cosine, sine_tab, factor):
    half_dim = values.shape[-1] // 2
    first_half = values[..., :half_dim]
    second = values[..., half_dim:]
    cosine = cosine[:, None, :]
    sine_tab = sine_tab[:, None, :]
    factor = factor[:, None, :]
    return jnp.concatenate(
        [
            (first_half * cosine - second * sine_tab) * factor,
            (second * cosine + first_half * sine_tab) * factor,
        ],
        axis=-1,
    )


def rotate_back(grad_rot, cosine, sine_tab, factor):
    half_dim = grad_rot.shape[-1] // 2
    first_half = grad_rot[..., :half_dim]
    second = grad_rot[..., half_dim:]
    cosine = cosine[:, None, :]
    sine_tab = sine_tab[:, None, :]
    factor = factor[:, None, :]
    return jnp.concatenate(
        [
            (first_half * cosine + second * sine_tab) * factor,
            (second * cosine - first_half * sine_tab) * factor,
        ],
        axis=-1,
    )


def plain_dot(first_op, second_op):
    return jnp.dot(first_op, second_op, preferred_element_type=jnp.float32)


def contract_last(first_op, second_op):
    return lax.dot_general(
        first_op, second_op, (((1,), (1,)), ((), ())), preferred_element_type=jnp.float32
    )


def contract_first(first_op, second_op):
    return lax.dot_general(
        first_op, second_op, (((0,), (0,)), ((), ())), preferred_element_type=jnp.float32
    )


class Ring:
    def __init__(self):
        self.devices = lax.axis_size("dp")
        self.chips = self.devices // 2
        half = self.chips // 2
        self.order = [2 * a for a in range(half)] + [2 * a + 1 for a in reversed(range(half))]
        self.index = lax.axis_index("dp")
        self.core = self.index % 2
        chip = self.index // 2
        self.place = jnp.where(chip % 2 == 0, chip // 2, self.chips - 1 - chip // 2)
        self.near = self.chips // 2
        self.far = self.chips - 1 - self.near

    def shift(self, rows, step):
        pairs = [
            (self.order[i] * 2 + c, self.order[(i + step) % self.chips] * 2 + c)
            for i in range(self.chips)
            for c in range(2)
        ]
        return lax.ppermute(rows, "dp", pairs)

    def swap(self, rows):
        return lax.ppermute(rows, "dp", [(i, i ^ 1) for i in range(self.devices)])

    def hops(self, flip):
        return (self.far, self.near) if flip else (self.near, self.far)

    def block_table(self):
        spot = (self.place + jnp.arange(self.chips, dtype=jnp.int32)) % self.chips
        chip = jnp.where(spot < self.chips // 2, 2 * spot, 2 * (self.chips - 1 - spot) + 1)
        return jnp.concatenate([chip * 2 + self.core, chip * 2 + 1 - self.core]).astype(jnp.int32)


class RingSum:
    def __init__(self, ring, full, arrived, flip):
        self.ring = ring
        self.full = full
        self.arrived = arrived
        self.block = full.shape[0] // ring.chips
        self.up, self.down = ring.hops(flip)
        self.moving = [
            self.term(k).astype(jnp.bfloat16) for k in (self.up, ring.chips - self.down)
        ]
        self.count = 0

    def term(self, k):
        rows = slice(k * self.block, (k + 1) * self.block)
        return self.full[rows].astype(jnp.float32) + self.arrived[rows].astype(jnp.float32)

    def step(self):
        ring = self.ring
        self.count += 1
        for way, hops, k in (
            (0, self.up, self.up - self.count),
            (1, self.down, ring.chips - self.down + self.count),
        ):
            if self.count <= hops:
                moved = ring.shift(self.moving[way], 1 - 2 * way)
                if self.count < hops:
                    moved = (moved.astype(jnp.float32) + self.term(k)).astype(jnp.bfloat16)
                self.moving[way] = moved

    def run(self, steps):
        for _ in range(min(steps, max(self.up, self.down) - self.count)):
            self.step()

    def result(self):
        self.run(self.ring.chips)
        return (
            self.term(0)
            + self.moving[0].astype(jnp.float32)
            + self.moving[1].astype(jnp.float32)
        )


def gather_ring(shards, call_id=1, first=None):
    devices = lax.axis_size("dp")
    chips = devices // 2
    half = chips // 2
    rows = shards[0].shape[0]
    count = len(shards)
    parts = 2
    piece = rows // parts
    hops = ((half, half - 1), (half - 1, half))

    def kernel(*refs):
        ins, refs = refs[:count], refs[count:]
        if first is not None:
            (blocks_ref, rows_ref), refs = refs[:2], refs[2:]
        outs, refs = refs[:count], refs[count:]
        if first is not None:
            (from_ref, norm_ref), refs = refs[:2], refs[2:]
        own_sem, side_send, side_recv, ring_send, ring_recv = refs[:5]
        index = lax.axis_index("dp")
        core, chip = index % 2, index // 2
        odd = chip % 2
        place = (1 - odd) * (chip // 2) + odd * (chips - 1 - chip // 2)

        def device_at(spot, which):
            spot = (spot + 2 * chips) % chips
            upper = spot // half
            there = (1 - upper) * (2 * spot) + upper * (2 * (chips - 1 - spot) + 1)
            return there * 2 + which

        def window(spot, which, part):
            first = device_at(spot, which) * rows + part * piece
            return pl.ds(pl.multiple_of(first, piece), piece)

        partner = chip * 2 + 1 - core
        neighbours = (device_at(place + 1, core), device_at(place - 1, core))

        if first is None:
            barrier = pltpu.get_barrier_semaphore()
            for target in (*neighbours, partner):
                pl.semaphore_signal(
                    barrier, inc=1, device_id={"dp": target}, device_id_type=pl.DeviceIdType.MESH
                )
            pl.semaphore_wait(barrier, 3)
        else:
            small = (blocks_ref, from_ref, refs[5], refs[6])
            exchange_start(*small)

        sends = []

        def source(j, spot, part, own):
            if own:
                return ins[j].at[pl.ds(part * piece, piece)]
            return outs[j].at[window(spot, core, part)]

        def ring_copy(j, way, part, hop):
            spot = place - (hop - 1) * (1 - 2 * way)
            return pltpu.make_async_remote_copy(
                src_ref=source(j, spot, part, hop == 1),
                dst_ref=outs[j].at[window(spot, core, part)],
                send_sem=ring_send.at[j, way, part, hop - 1],
                recv_sem=ring_recv.at[j, way, part, hop - 1],
                device_id={"dp": neighbours[way]},
                device_id_type=pl.DeviceIdType.MESH,
            )

        def ring_arrival(j, way, part, hop):
            spot = place - hop * (1 - 2 * way)
            here = outs[j].at[window(spot, core, part)]
            return pltpu.make_async_remote_copy(
                src_ref=here,
                dst_ref=here,
                send_sem=ring_send.at[j, way, part, hop - 1],
                recv_sem=ring_recv.at[j, way, part, hop - 1],
                device_id={"dp": neighbours[way]},
                device_id_type=pl.DeviceIdType.MESH,
            )

        def side_copy(j, part, slot, spot, own):
            return pltpu.make_async_remote_copy(
                src_ref=source(j, spot, part, own),
                dst_ref=outs[j].at[window(spot, core, part)],
                send_sem=side_send.at[j, part, slot],
                recv_sem=side_recv.at[j, part, slot],
                device_id={"dp": partner},
                device_id_type=pl.DeviceIdType.MESH,
            )

        def side_arrival(j, part, slot, spot):
            here = outs[j].at[window(spot, 1 - core, part)]
            return pltpu.make_async_remote_copy(
                src_ref=here,
                dst_ref=here,
                send_sem=side_send.at[j, part, slot],
                recv_sem=side_recv.at[j, part, slot],
                device_id={"dp": partner},
                device_id_type=pl.DeviceIdType.MESH,
            )

        def launch(copy):
            copy.start()
            sends.append(copy)

        for part in range(parts):
            for j in range(count):
                for way in range(2):
                    launch(ring_copy(j, way, part, 1))
        owns = []
        for part in range(parts):
            for j in range(count):
                launch(side_copy(j, part, 0, place, True))
                own = pltpu.make_async_copy(
                    source(j, place, part, True),
                    outs[j].at[window(place, core, part)],
                    own_sem.at[j, part],
                )
                own.start()
                owns.append(own)
        if first is not None:
            exchange_finish(*small)
            values = rows_ref[...].astype(jnp.float32)
            normed, _ = norm_stats(values, EPSILON)
            mp_size = lax.axis_size("mp")
            for d in range(devices):
                cols = slice(d * rows, (d + 1) * rows)
                sent = from_ref[d * mp_size]
                norm_ref[0, :, cols] = (normed[:, cols] * sent[0:1] + sent[1:2]).astype(
                    norm_ref.dtype
                )
        for hop in range(1, half + 1):
            if first is not None and hop == 2:
                across = pltpu.make_async_remote_copy(
                    src_ref=norm_ref.at[0],
                    dst_ref=norm_ref.at[1],
                    send_sem=refs[7].at[0],
                    recv_sem=refs[7].at[1],
                    device_id={"mp": 1 - lax.axis_index("mp")},
                    device_id_type=pl.DeviceIdType.MESH,
                )
                across.start()
            for part in range(parts):
                for j in range(count):
                    for way in range(2):
                        if hop <= hops[way][part]:
                            ring_arrival(j, way, part, hop).wait_recv()
                            if hop < hops[way][part]:
                                launch(ring_copy(j, way, part, hop + 1))
                            turn = 1 - 2 * way
                            slot = (chips - hop * turn) % chips
                            launch(side_copy(j, part, slot, place - hop * turn, False))
        for own in owns:
            own.wait()
        for copy in sends:
            copy.wait_send()
        for slot in range(chips):
            for part in range(parts):
                for j in range(count):
                    side_arrival(j, part, slot, place + slot).wait_recv()
        if first is not None:
            across.wait()

    total = sum(shard.shape[1] for shard in shards) * rows * 2
    out_shape = [
        jax.ShapeDtypeStruct((devices * rows, shard.shape[1]), shard.dtype) for shard in shards
    ]
    in_specs = [pl.BlockSpec(memory_space=pl.ANY)] * count
    out_specs = [pl.BlockSpec(memory_space=pl.ANY)] * count
    scratch = [
        pltpu.SemaphoreType.DMA((count, parts)),
        pltpu.SemaphoreType.DMA((count, parts, chips)),
        pltpu.SemaphoreType.DMA((count, parts, chips)),
        pltpu.SemaphoreType.DMA((count, 2, parts, half)),
        pltpu.SemaphoreType.DMA((count, 2, parts, half)),
    ]
    extra = ()
    if first is not None:
        extra = first
        peers = devices * lax.axis_size("mp")
        in_specs = in_specs + [pl.BlockSpec(memory_space=pltpu.VMEM)] * 2
        out_specs = out_specs + [pl.BlockSpec(memory_space=pltpu.VMEM)] * 2
        out_shape = out_shape + [
            jax.ShapeDtypeStruct((peers, *first[0].shape[1:]), first[0].dtype),
            jax.ShapeDtypeStruct((2, *first[1].shape), jnp.bfloat16),
        ]
        scratch = scratch + [
            pltpu.SemaphoreType.DMA((peers,)),
            pltpu.SemaphoreType.DMA((peers,)),
            pltpu.SemaphoreType.DMA((2,)),
        ]
    return pl.pallas_call(
        kernel,
        out_shape=out_shape,
        in_specs=in_specs,
        out_specs=out_specs,
        scratch_shapes=scratch,
        compiler_params=pltpu.CompilerParams(collective_id=call_id, has_side_effects=True),
        cost_estimate=pl.CostEstimate(
            flops=0, bytes_accessed=total * devices * 4, transcendentals=0
        ),
    )(*shards, *extra)


def ring_total(rows):
    devices = lax.axis_size("dp")
    chips = devices // 2
    half = chips // 2
    hops = (half, chips - 1 - half)
    width = rows.shape[1]
    piece = rows.shape[0] // (2 * chips)
    low = rows.dtype

    def kernel(
        in_ref,
        out_ref,
        mate,
        mine,
        landed,
        packed,
        pair_sem,
        sum_send,
        sum_recv,
        ring_send,
        ring_recv,
        side_send,
        side_recv,
    ):
        index = lax.axis_index("dp")
        core, chip = index % 2, index // 2
        odd = chip % 2
        place = (1 - odd) * (chip // 2) + odd * (chips - 1 - chip // 2)

        def device_at(spot):
            spot = (spot + 2 * chips) % chips
            upper = spot // half
            there = (1 - upper) * (2 * spot) + upper * (2 * (chips - 1 - spot) + 1)
            return there * 2 + core

        def spot(k):
            return (place + k + 2 * chips) % chips

        partner = chip * 2 + 1 - core
        neighbours = (device_at(place + 1), device_at(place - 1))

        def copy_to(target, source, dest, send, recv):
            return pltpu.make_async_remote_copy(
                src_ref=source,
                dst_ref=dest,
                send_sem=send,
                recv_sem=recv,
                device_id={"dp": target},
                device_id_type=pl.DeviceIdType.MESH,
            )

        barrier = pltpu.get_barrier_semaphore()
        for target in (*neighbours, partner):
            pl.semaphore_signal(
                barrier, inc=1, device_id={"dp": target}, device_id_type=pl.DeviceIdType.MESH
            )
        pl.semaphore_wait(barrier, 3)

        pair = copy_to(partner, in_ref.at[1 - core], mate, pair_sem.at[0], pair_sem.at[1])
        pair.start()
        pair.wait()

        def add_mate(k, carry):
            mine[k] = (in_ref[core, k].astype(jnp.float32) + mate[k].astype(jnp.float32)).astype(
                low
            )
            return carry

        lax.fori_loop(0, chips, add_mate, 0)

        sends = []

        def launch(copy):
            copy.start()
            sends.append(copy)

        def sum_copy(way, step, source):
            return copy_to(
                neighbours[way],
                source,
                landed.at[way, step],
                sum_send.at[way, step],
                sum_recv.at[way, step],
            )

        for way in range(2):
            launch(sum_copy(way, 0, mine.at[spot(hops[way] * (1 - 2 * way))]))
        for step in range(1, half + 1):
            for way in range(2):
                if step <= hops[way]:
                    sum_copy(way, step - 1, landed.at[way, step - 1]).wait_recv()
                    if step < hops[way]:
                        ahead = spot((hops[way] - step) * (1 - 2 * way))
                        packed[way, step] = (
                            landed[way, step - 1].astype(jnp.float32)
                            + mine[ahead].astype(jnp.float32)
                        ).astype(low)
                        launch(sum_copy(way, step, packed.at[way, step]))
        out_ref[core, place] = (
            mine[place].astype(jnp.float32)
            + landed[0, hops[0] - 1].astype(jnp.float32)
            + landed[1, hops[1] - 1].astype(jnp.float32)
        ).astype(low)

        def ring_copy(way, hop):
            there = out_ref.at[core, spot(-(hop - 1) * (1 - 2 * way))]
            return copy_to(
                neighbours[way], there, there, ring_send.at[way, hop - 1], ring_recv.at[way, hop - 1]
            )

        def ring_arrival(way, hop):
            here = out_ref.at[core, spot(-hop * (1 - 2 * way))]
            return copy_to(
                neighbours[way], here, here, ring_send.at[way, hop - 1], ring_recv.at[way, hop - 1]
            )

        def side_copy(slot, which):
            there = out_ref.at[which, spot(slot)]
            return copy_to(partner, there, there, side_send.at[slot], side_recv.at[slot])

        for way in range(2):
            launch(ring_copy(way, 1))
        launch(side_copy(0, core))
        for hop in range(1, half + 1):
            for way in range(2):
                if hop <= hops[way]:
                    ring_arrival(way, hop).wait_recv()
                    if hop < hops[way]:
                        launch(ring_copy(way, hop + 1))
                    launch(side_copy((chips - hop * (1 - 2 * way)) % chips, core))
        for copy in sends:
            copy.wait_send()
        for slot in range(chips):
            side_copy(slot, 1 - core).wait_recv()

    shape = (2, chips, piece, width)
    total = pl.pallas_call(
        kernel,
        out_shape=jax.ShapeDtypeStruct(shape, low),
        in_specs=[pl.BlockSpec(memory_space=pltpu.VMEM)],
        out_specs=pl.BlockSpec(memory_space=pltpu.VMEM),
        scratch_shapes=[
            pltpu.VMEM(shape[1:], low),
            pltpu.VMEM(shape[1:], low),
            pltpu.VMEM((2, half, piece, width), low),
            pltpu.VMEM((2, half, piece, width), low),
            pltpu.SemaphoreType.DMA((2,)),
            pltpu.SemaphoreType.DMA((2, half)),
            pltpu.SemaphoreType.DMA((2, half)),
            pltpu.SemaphoreType.DMA((2, half)),
            pltpu.SemaphoreType.DMA((2, half)),
            pltpu.SemaphoreType.DMA((chips,)),
            pltpu.SemaphoreType.DMA((chips,)),
        ],
        compiler_params=pltpu.CompilerParams(collective_id=5, has_side_effects=True),
    )(rows.reshape(shape))
    return total.reshape(rows.shape)


def each_peer(action):
    dp_size, mp_size = lax.axis_size("dp"), lax.axis_size("mp")
    me = lax.axis_index("dp") * mp_size + lax.axis_index("mp")
    for place in range(dp_size * mp_size):
        pl.when(me != place)(
            functools.partial(action, place, place // mp_size, place % mp_size)
        )


def exchange_start(in_ref, out_ref, send_sem, recv_sem):
    dp_size, mp_size = lax.axis_size("dp"), lax.axis_size("mp")
    dp_index = lax.axis_index("dp")
    me = dp_index * mp_size + lax.axis_index("mp")
    barrier = pltpu.get_barrier_semaphore()

    def greet(place, row, col):
        pl.semaphore_signal(
            barrier, inc=1, device_id=(row, col), device_id_type=pl.DeviceIdType.MESH
        )

    each_peer(greet)
    pl.semaphore_wait(barrier, dp_size * mp_size - 1)

    def send(place, row, col):
        pltpu.make_async_remote_copy(
            src_ref=in_ref.at[row],
            dst_ref=out_ref.at[me],
            send_sem=send_sem.at[place],
            recv_sem=recv_sem.at[me],
            device_id=(row, col),
            device_id_type=pl.DeviceIdType.MESH,
        ).start()

    each_peer(send)
    out_ref[me] = in_ref[dp_index]


def exchange_finish(in_ref, out_ref, send_sem, recv_sem):
    def finish(place, row, col):
        copy = pltpu.make_async_remote_copy(
            src_ref=in_ref.at[row],
            dst_ref=out_ref.at[place],
            send_sem=send_sem.at[place],
            recv_sem=recv_sem.at[place],
            device_id=(row, col),
            device_id_type=pl.DeviceIdType.MESH,
        )
        copy.wait_send()
        copy.wait_recv()

    each_peer(finish)


def exchange_blocks(blocks):
    dp_size, mp_size = lax.axis_size("dp"), lax.axis_size("mp")
    total = dp_size * mp_size

    def kernel(in_ref, out_ref, send_sem, recv_sem):
        exchange_start(in_ref, out_ref, send_sem, recv_sem)
        exchange_finish(in_ref, out_ref, send_sem, recv_sem)

    return pl.pallas_call(
        kernel,
        out_shape=jax.ShapeDtypeStruct((total, *blocks.shape[1:]), blocks.dtype),
        in_specs=[pl.BlockSpec(memory_space=pltpu.VMEM)],
        out_specs=pl.BlockSpec(memory_space=pltpu.VMEM),
        scratch_shapes=[
            pltpu.SemaphoreType.DMA((total,)),
            pltpu.SemaphoreType.DMA((total,)),
        ],
        compiler_params=pltpu.CompilerParams(collective_id=2, has_side_effects=True),
    )(blocks)


def move_blocks(rows, table, outward):
    blocks = table.shape[0]
    width = rows.shape[1] // blocks

    def kernel(table_ref, in_ref, out_ref):
        for place in range(blocks):
            there = pl.ds(pl.multiple_of(table_ref[place] * width, width), width)
            here = pl.ds(place * width, width)
            if outward:
                out_ref[:, there] = in_ref[:, here]
            else:
                out_ref[:, here] = in_ref[:, there]

    if width % 128:
        order = table
        if outward:
            order = jnp.sum(
                jnp.where(table[None, :] == jnp.arange(blocks)[:, None], jnp.arange(blocks), 0),
                axis=1,
            )
        return jnp.take(rows.reshape(rows.shape[0], blocks, width), order, axis=1).reshape(
            rows.shape
        )
    return pl.pallas_call(
        kernel,
        out_shape=jax.ShapeDtypeStruct(rows.shape, rows.dtype),
        in_specs=[
            pl.BlockSpec(memory_space=pltpu.SMEM),
            pl.BlockSpec(memory_space=pltpu.VMEM),
        ],
        out_specs=pl.BlockSpec(memory_space=pltpu.VMEM),
    )(table, rows)


def swap_mp(rows):
    return lax.ppermute(rows, "mp", [(0, 1), (1, 0)])


def gather_rows(rows_low):
    return jnp.concatenate([rows_low, swap_mp(rows_low)], axis=0)


def scatter_rows(terms):
    half_rows = terms.shape[0] // 2
    arrived = swap_mp(terms[half_rows:].astype(jnp.bfloat16))
    return terms[:half_rows] + arrived.astype(jnp.float32)


def tie(value, other):
    return lax.optimization_barrier((value, other))[0]


def on_device(
    tokens_in,
    teacher,
    valid_mask,
    group_of,
    prompt_len,
    ln1_gain,
    ln1_bias,
    w_query,
    w_key,
    w_value,
    w_gate,
    w_out,
    ln2_gain,
    ln2_bias,
    w_up,
    w_down,
):
    half_rows = tokens_in.shape[0]
    model_dim = tokens_in.shape[1]
    seg_len = half_rows * lax.axis_size("mp")
    seg_count = group_of.shape[0]
    group_count = prompt_len.shape[0]
    heads_local = w_query.shape[1] // DK
    token_total = seg_len * seg_count
    dp_index = lax.axis_index("dp")
    mp_index = lax.axis_index("mp")
    ring = Ring()
    own_width = model_dim // 2
    table = ring.block_table()

    segment_ids = jnp.arange(seg_count, dtype=jnp.int32)
    my_group = jnp.sum(jnp.where(segment_ids == dp_index, group_of, 0))
    first_member = jnp.min(jnp.where(group_of == my_group, segment_ids, seg_count))
    prompt_flag = (first_member == dp_index).astype(jnp.float32)
    group_match = jnp.arange(group_count, dtype=jnp.int32) == my_group
    group_onehot = group_match.astype(jnp.float32)
    prompt_size = jnp.sum(jnp.where(group_match, prompt_len, 0))
    own_ids = mp_index * half_rows + jnp.arange(half_rows, dtype=jnp.int32)
    other_ids = (1 - mp_index) * half_rows + jnp.arange(half_rows, dtype=jnp.int32)
    token_ids = jnp.concatenate([own_ids, other_ids])
    loss_mask = valid_mask[0].astype(jnp.float32) * jnp.where(
        prompt_flag > 0, own_ids < prompt_size, True
    ).astype(jnp.float32)
    block = model_dim // ring.devices

    def packed(rows, scalar):
        split = rows.reshape(rows.shape[0], -1, block).transpose(1, 0, 2)
        split = jnp.pad(split, ((0, 0), (0, 0), (0, 128 - block)))
        extra = jnp.broadcast_to(scalar, (split.shape[0], 8 - rows.shape[0], 128))
        return jnp.concatenate([split, extra], axis=1)

    vectors = jnp.stack([ln1_gain, ln1_bias, ln2_gain, ln2_bias]).astype(jnp.float32)
    blocks_own = packed(jnp.tile(vectors, (1, ring.devices)), jnp.sum(loss_mask))
    inside = block == 128
    if inside:
        wk_full, wv_full, from_all, a_pair = gather_ring(
            [w_key, w_value], 1, (blocks_own, tokens_in)
        )
        a_all = a_pair.reshape(seg_len, model_dim)
    else:
        from_all = exchange_blocks(blocks_own)
    valid_count = jnp.sum(from_all[:, 4, 0])
    by_row = from_all.reshape(ring.devices, -1, 8, 128)[:, 0, :4, :block]
    gain_one, bias_one, gain_two, bias_two = (
        by_row[:, i].reshape(1, model_dim) for i in range(4)
    )

    def gather_all(shard):
        return lax.all_gather(shard, "dp", axis=0, tiled=True)

    offset = jnp.where(prompt_flag > 0, 0, prompt_size)
    positions = (token_ids + offset).astype(jnp.float32)
    head_ids = (mp_index * heads_local + jnp.arange(heads_local, dtype=jnp.int32)).astype(
        jnp.float32
    )
    log_decay = jnp.log(1.0 - 2.0 ** (-5.0 - head_ids))
    before_end = token_ids < prompt_size
    state_age = (prompt_size - 1 - token_ids).astype(jnp.float32)
    state_weighting = jnp.where(
        (before_end & (prompt_flag > 0))[:, None],
        jnp.exp(log_decay[None, :] * jnp.maximum(state_age, 0.0)[:, None]),
        0.0,
    )
    float_ids = token_ids.astype(jnp.float32)
    continuation_factor = (1.0 - prompt_flag) * jnp.exp(
        log_decay[None, :] * (float_ids + 1.0)[:, None]
    )
    distance = float_ids[:, None] - float_ids[None, :]
    decay_mat = jnp.where(
        distance[None] >= 0.0,
        jnp.exp(log_decay[:, None, None] * jnp.maximum(distance, 0.0)[None]),
        0.0,
    )
    token_rows = tokens_in.astype(jnp.float32)
    teacher_rows = teacher.astype(jnp.float32)
    normed_one, inv_one = norm_stats(token_rows, EPSILON)
    if not inside:
        a_all = gather_rows((normed_one * gain_one + bias_one).astype(jnp.bfloat16))
        wk_full, wv_full = gather_ring([w_key, w_value])
    keys_raw = lax.optimization_barrier(plain_dot(a_all, wk_full)).reshape(seg_len, heads_local, DK)
    reduced_values = (
        plain_dot(a_all, wv_full).astype(jnp.bfloat16).reshape(seg_len, heads_local, DV)
    )
    cosine, sine_tab, grow_fac = xpos_tables(positions, 1.0)
    _, _, shrink = xpos_tables(positions, -1.0)
    q_scale = DK ** (-0.5)
    rotated_keys = rotate_pairs(keys_raw, cosine, sine_tab, shrink).astype(jnp.bfloat16)
    local_state = jnp.einsum(
        "jld,jla->lda",
        (rotated_keys.astype(jnp.float32) * state_weighting[:, :, None]).astype(jnp.bfloat16),
        reduced_values,
        preferred_element_type=jnp.float32,
    )
    slots = (group_onehot[:, None, None, None] * (prompt_flag * local_state)[None]).astype(
        jnp.bfloat16
    )
    summed = lax.psum(slots, "dp")
    wq_full, wg_full, wo_full = gather_ring([tie(w_query, slots), w_gate, w_out], 3)
    wd_full = gather_all(tie(w_down, (wq_full, summed)))
    state_lookup = jnp.sum(
        summed.astype(jnp.float32) * group_onehot[:, None, None, None], axis=0
    ).astype(jnp.bfloat16)
    queries = lax.optimization_barrier(plain_dot(a_all, wq_full)).reshape(seg_len, heads_local, DK)
    gate_pre = plain_dot(a_all, wg_full)
    rotated_queries = (rotate_pairs(queries, cosine, sine_tab, grow_fac) * q_scale).astype(
        jnp.bfloat16
    )
    scores = jnp.einsum(
        "thk,nhk->htn", rotated_queries, rotated_keys, preferred_element_type=jnp.float32
    )
    weights_low = (scores * decay_mat).astype(jnp.bfloat16)
    retained_output = jnp.einsum(
        "htn,nhv->thv", weights_low, reduced_values, preferred_element_type=jnp.float32
    )
    carried_forward = jnp.einsum(
        "ozi,ziw->ozw", rotated_queries, state_lookup, preferred_element_type=jnp.float32
    )
    retained_output = retained_output + continuation_factor[:, :, None] * carried_forward
    grouped, inv_group = norm_stats(retained_output, GROUP_EPSILON)
    gate_act = jax.nn.silu(gate_pre).reshape(seg_len, heads_local, DV)
    gated_out = (gate_act * grouped).reshape(seg_len, heads_local * DV).astype(jnp.bfloat16)
    attn_own = scatter_rows(contract_last(gated_out, wo_full))
    hidden_res = token_rows + attn_own
    normed_two, inv_two = norm_stats(hidden_res, EPSILON)
    c_own = (normed_two * gain_two + bias_two).astype(jnp.bfloat16)
    c_all = gather_rows(c_own)
    (wu_full,) = gather_ring([tie(w_up, c_own)], 4)
    up_pre = plain_dot(c_all, wu_full)
    up_act = jax.nn.gelu(up_pre, approximate=False).astype(jnp.bfloat16)
    ffn_own = scatter_rows(contract_last(up_act, wd_full))
    block_out = hidden_res + ffn_own
    error_rows = block_out - teacher_rows
    weighted = loss_mask[:, None] * error_rows
    squared_own = jnp.sum(weighted * error_rows)
    grad_out = token_total / valid_count * weighted

    def weight_grad(feature_side, other_side, flip):
        keep = contract_first(feature_side[:, :own_width], other_side).astype(jnp.bfloat16)
        give = contract_first(feature_side[:, own_width:], other_side).astype(jnp.bfloat16)
        return RingSum(ring, keep, ring.swap(give), flip)

    def in_order(rows):
        return move_blocks(rows, table, False)

    def then(value, *ring_sums):
        return tie(value, tuple(r.moving[way] for r in ring_sums for way in range(2)))

    grad_ffn_all = gather_rows(grad_out.astype(jnp.bfloat16))
    sum_wd = weight_grad(in_order(grad_ffn_all), up_act, False)
    grad_up_act = plain_dot(tie(grad_ffn_all, sum_wd.full), wd_full)
    _, gelu_pull = jax.vjp(lambda inner: jax.nn.gelu(inner, approximate=False), up_pre)
    grad_up = gelu_pull(grad_up_act)[0].astype(jnp.bfloat16)
    sum_wu = weight_grad(in_order(c_all), grad_up, True)
    sum_wd.run(1)
    grad_up = tie(then(grad_up, sum_wd), sum_wu.full)
    grad_c_parts = contract_last(grad_up, wu_full)
    grad_c = scatter_rows(grad_c_parts)
    sum_wd.run(1)
    grad_c = then(grad_c, sum_wd)
    grad_gain2_part = jnp.sum(grad_c * normed_two, axis=0)
    grad_bias2_part = jnp.sum(grad_c, axis=0)
    grad_hidden = grad_out + norm_back(grad_c * gain_two, normed_two, inv_two)
    grad_attn_all = gather_rows(grad_hidden.astype(jnp.bfloat16))
    sum_wd.run(2)
    sum_wu.run(1)
    grad_attn_all = then(grad_attn_all, sum_wd, sum_wu)
    sum_wo = weight_grad(in_order(grad_attn_all), gated_out, False)
    grad_attn_all = tie(grad_attn_all, sum_wo.full)
    grad_gated = plain_dot(grad_attn_all, wo_full).reshape(seg_len, heads_local, DV)
    _, silu_pull = jax.vjp(jax.nn.silu, gate_pre)
    grad_gate = silu_pull((grad_gated * grouped).reshape(seg_len, heads_local * DV))[0].astype(
        jnp.bfloat16
    )
    retained_gradient = norm_back(grad_gated * gate_act, grouped, inv_group).astype(jnp.bfloat16)
    state_grad_own = jnp.einsum(
        "ybn,ybw->bnw",
        (rotated_queries.astype(jnp.float32) * continuation_factor[:, :, None]).astype(
            jnp.bfloat16
        ),
        retained_gradient,
        preferred_element_type=jnp.float32,
    )
    grad_slots = (group_onehot[:, None, None, None] * state_grad_own[None]).astype(jnp.bfloat16)
    grad_summed = ring_total(grad_slots.reshape(-1, DV)).reshape(grad_slots.shape)
    retained_gradient = tie(retained_gradient, grad_summed)
    sum_wu.run(2)
    a_order = in_order(a_all)
    grad_gate = then(grad_gate, sum_wu)
    sum_wg = weight_grad(a_order, grad_gate, True)
    retained_gradient = tie(retained_gradient, sum_wg.full)
    sum_wu.run(1)
    sum_wo.run(1)
    grad_weights = jnp.einsum(
        "thv,nhv->htn", retained_gradient, reduced_values, preferred_element_type=jnp.float32
    )
    grad_values = jnp.einsum(
        "htn,thv->nhv", weights_low, retained_gradient, preferred_element_type=jnp.float32
    )
    grad_scores = then((grad_weights * decay_mat).astype(jnp.bfloat16), sum_wu, sum_wo)
    sum_wo.run(1)
    grad_q_rot = jnp.einsum(
        "htn,nhk->thk", grad_scores, rotated_keys, preferred_element_type=jnp.float32
    )
    grad_q_rot = grad_q_rot + continuation_factor[:, :, None] * jnp.einsum(
        "mjr,jwr->mjw", retained_gradient, state_lookup, preferred_element_type=jnp.float32
    )
    grad_k_rot = jnp.einsum(
        "htn,thk->nhk", grad_scores, rotated_queries, preferred_element_type=jnp.float32
    )
    grad_queries = (
        rotate_back(grad_q_rot * q_scale, cosine, sine_tab, grow_fac)
        .reshape(seg_len, heads_local * DK)
        .astype(jnp.bfloat16)
    )
    grad_queries = then(grad_queries, sum_wo)
    sum_wq = weight_grad(a_order, grad_queries, False)
    state_gradient = (
        prompt_flag
        * jnp.sum(grad_summed.astype(jnp.float32) * group_onehot[:, None, None, None], axis=0)
    ).astype(jnp.bfloat16)
    grad_k_rot = grad_k_rot + state_weighting[:, :, None] * jnp.einsum(
        "ilm,lpm->ilp", reduced_values, state_gradient, preferred_element_type=jnp.float32
    )
    grad_values = grad_values + state_weighting[:, :, None] * jnp.einsum(
        "zdo,doi->zdi", rotated_keys, state_gradient, preferred_element_type=jnp.float32
    )
    grad_keys = (
        rotate_back(grad_k_rot, cosine, sine_tab, shrink)
        .reshape(seg_len, heads_local * DK)
        .astype(jnp.bfloat16)
    )
    grad_vlow = grad_values.reshape(seg_len, heads_local * DV).astype(jnp.bfloat16)
    grad_key_value = jnp.concatenate([grad_keys, grad_vlow], axis=1)
    sum_wkv = weight_grad(a_order, grad_key_value, True)
    grad_keys = tie(grad_keys, sum_wkv.arrived)
    grad_a = scatter_rows(
        contract_last(grad_queries, wq_full)
        + contract_last(grad_gate, wg_full)
        + contract_last(grad_keys, wk_full)
        + contract_last(grad_vlow, wv_full)
    )
    sum_wo.run(2)
    sum_wg.run(1)
    grad_gain1_part = jnp.sum(grad_a * normed_one, axis=0)
    grad_bias1_part = jnp.sum(grad_a, axis=0)
    grad_tokens = grad_hidden + norm_back(grad_a * gain_one, normed_one, inv_one)

    sums = jnp.stack([grad_gain1_part, grad_bias1_part, grad_gain2_part, grad_bias2_part])
    totals = jnp.sum(exchange_blocks(packed(sums, squared_own)), axis=0)
    loss_value = totals[4, 0] / (valid_count * model_dim)
    key_width = w_key.shape[1]
    sum_wg.run(2)
    sum_wg.moving = [tie(x, totals) for x in sum_wg.moving]
    grad_wkv = sum_wkv.result()

    return (
        block_out,
        grad_tokens,
        loss_value,
        totals[0, :block],
        totals[1, :block],
        sum_wq.result(),
        grad_wkv[:, :key_width],
        grad_wkv[:, key_width:],
        sum_wg.result(),
        sum_wo.result(),
        totals[2, :block],
        totals[3, :block],
        sum_wu.result(),
        sum_wd.result(),
    )


def solution(mesh):
    return jax.shard_map(
        on_device,
        mesh=mesh,
        in_specs=(
            P(("dp", "mp"), None),
            P(("dp", "mp"), None),
            P("dp", "mp"),
            P(),
            P(),
            P("dp"),
            P("dp"),
            P("dp", "mp"),
            P("dp", "mp"),
            P("dp", "mp"),
            P("dp", "mp"),
            P("dp", "mp"),
            P("dp"),
            P("dp"),
            P("dp", "mp"),
            P("dp", "mp"),
        ),
        out_specs=(
            P(("dp", "mp"), None),
            P(("dp", "mp"), None),
            P(),
            P("dp"),
            P("dp"),
            P("dp", "mp"),
            P("dp", "mp"),
            P("dp", "mp"),
            P("dp", "mp"),
            P("dp", "mp"),
            P("dp"),
            P("dp"),
            P("dp", "mp"),
            P("dp", "mp"),
        ),
        check_vma=False,
    )
```

```python
import functools
import math

import jax
import jax.numpy as jnp
from jax import lax
from jax.experimental import pallas as pl
from jax.experimental.pallas import tpu as pltpu
from jax.sharding import PartitionSpec as P

DK = 256
DV = 512


EPSILON = 1e-05
GROUP_EPSILON = 0.05


def norm_stats(values, floor_eps):
    center = jnp.mean(values, axis=-1, keepdims=True)
    shifted = values - center
    inv_std = lax.rsqrt(jnp.mean(shifted * shifted, axis=-1, keepdims=True) + floor_eps)
    return (shifted * inv_std, inv_std)


def norm_back(grad_in, normed, inv_std):
    mean_grad = jnp.mean(grad_in, axis=-1, keepdims=True)
    mean_proj = jnp.mean(grad_in * normed, axis=-1, keepdims=True)
    return (grad_in - mean_grad - normed * mean_proj) * inv_std


def xpos_tables(positions, direction):
    half_dim = DK // 2
    pair_index = jnp.arange(half_dim, dtype=jnp.float32)
    frequency = jnp.exp(-(2.0 * pair_index / DK) * math.log(10000.0))
    base_ratio = (2.0 * pair_index / DK + 0.4) / 1.4
    angles = positions[:, None] * frequency[None, :]
    factor = jnp.exp(direction * (positions[:, None] / 512.0) * jnp.log(base_ratio)[None, :])
    return (jnp.cos(angles), jnp.sin(angles), factor)


def rotate_pairs(values, cosine, sine_tab, factor):
    half_dim = values.shape[-1] // 2
    first_half = values[..., :half_dim]
    second = values[..., half_dim:]
    cosine = cosine[:, None, :]
    sine_tab = sine_tab[:, None, :]
    factor = factor[:, None, :]
    return jnp.concatenate(
        [
            (first_half * cosine - second * sine_tab) * factor,
            (second * cosine + first_half * sine_tab) * factor,
        ],
        axis=-1,
    )


def rotate_back(grad_rot, cosine, sine_tab, factor):
    half_dim = grad_rot.shape[-1] // 2
    first_half = grad_rot[..., :half_dim]
    second = grad_rot[..., half_dim:]
    cosine = cosine[:, None, :]
    sine_tab = sine_tab[:, None, :]
    factor = factor[:, None, :]
    return jnp.concatenate(
        [
            (first_half * cosine + second * sine_tab) * factor,
            (second * cosine - first_half * sine_tab) * factor,
        ],
        axis=-1,
    )


def plain_dot(first_op, second_op):
    return jnp.dot(first_op, second_op, preferred_element_type=jnp.float32)


def contract_last(first_op, second_op):
    return lax.dot_general(
        first_op, second_op, (((1,), (1,)), ((), ())), preferred_element_type=jnp.float32
    )


def contract_first(first_op, second_op):
    return lax.dot_general(
        first_op, second_op, (((0,), (0,)), ((), ())), preferred_element_type=jnp.float32
    )


class Ring:
    def __init__(self):
        self.devices = lax.axis_size("dp")
        self.chips = self.devices // 2
        half = self.chips // 2
        self.order = [2 * a for a in range(half)] + [2 * a + 1 for a in reversed(range(half))]
        self.index = lax.axis_index("dp")
        self.core = self.index % 2
        chip = self.index // 2
        self.place = jnp.where(chip % 2 == 0, chip // 2, self.chips - 1 - chip // 2)
        self.near = self.chips // 2
        self.far = self.chips - 1 - self.near

    def shift(self, rows, step):
        pairs = [
            (self.order[i] * 2 + c, self.order[(i + step) % self.chips] * 2 + c)
            for i in range(self.chips)
            for c in range(2)
        ]
        return lax.ppermute(rows, "dp", pairs)

    def swap(self, rows):
        return lax.ppermute(rows, "dp", [(i, i ^ 1) for i in range(self.devices)])

    def hops(self, flip):
        return (self.far, self.near) if flip else (self.near, self.far)

    def block_table(self):
        spot = (self.place + jnp.arange(self.chips, dtype=jnp.int32)) % self.chips
        chip = jnp.where(spot < self.chips // 2, 2 * spot, 2 * (self.chips - 1 - spot) + 1)
        return jnp.concatenate([chip * 2 + self.core, chip * 2 + 1 - self.core]).astype(jnp.int32)


class RingSum:
    def __init__(self, ring, full, arrived, flip):
        self.ring = ring
        self.full = full
        self.arrived = arrived
        self.block = full.shape[0] // ring.chips
        self.up, self.down = ring.hops(flip)
        self.moving = [
            self.term(k).astype(jnp.bfloat16) for k in (self.up, ring.chips - self.down)
        ]
        self.count = 0

    def term(self, k):
        rows = slice(k * self.block, (k + 1) * self.block)
        return self.full[rows].astype(jnp.float32) + self.arrived[rows].astype(jnp.float32)

    def step(self):
        ring = self.ring
        self.count += 1
        for way, hops, k in (
            (0, self.up, self.up - self.count),
            (1, self.down, ring.chips - self.down + self.count),
        ):
            if self.count <= hops:
                moved = ring.shift(self.moving[way], 1 - 2 * way)
                if self.count < hops:
                    moved = (moved.astype(jnp.float32) + self.term(k)).astype(jnp.bfloat16)
                self.moving[way] = moved

    def run(self, steps):
        for _ in range(min(steps, max(self.up, self.down) - self.count)):
            self.step()

    def result(self):
        self.run(self.ring.chips)
        return (
            self.term(0)
            + self.moving[0].astype(jnp.float32)
            + self.moving[1].astype(jnp.float32)
        )


def gather_ring(shards, call_id=1, first=None):
    devices = lax.axis_size("dp")
    chips = devices // 2
    half = chips // 2
    rows = shards[0].shape[0]
    count = len(shards)
    parts = 2
    piece = rows // parts
    hops = ((half, half - 1), (half - 1, half))

    def kernel(*refs):
        ins, refs = refs[:count], refs[count:]
        if first is not None:
            (blocks_ref, rows_ref), refs = refs[:2], refs[2:]
        outs, refs = refs[:count], refs[count:]
        if first is not None:
            (from_ref, norm_ref), refs = refs[:2], refs[2:]
        own_sem, side_send, side_recv, ring_send, ring_recv = refs[:5]
        index = lax.axis_index("dp")
        core, chip = index % 2, index // 2
        odd = chip % 2
        place = (1 - odd) * (chip // 2) + odd * (chips - 1 - chip // 2)

        def device_at(spot, which):
            spot = (spot + 2 * chips) % chips
            upper = spot // half
            there = (1 - upper) * (2 * spot) + upper * (2 * (chips - 1 - spot) + 1)
            return there * 2 + which

        def window(spot, which, part):
            first = device_at(spot, which) * rows + part * piece
            return pl.ds(pl.multiple_of(first, piece), piece)

        partner = chip * 2 + 1 - core
        neighbours = (device_at(place + 1, core), device_at(place - 1, core))

        if first is None:
            barrier = pltpu.get_barrier_semaphore()
            for target in (*neighbours, partner):
                pl.semaphore_signal(
                    barrier, inc=1, device_id={"dp": target}, device_id_type=pl.DeviceIdType.MESH
                )
            pl.semaphore_wait(barrier, 3)
        else:
            small = (blocks_ref, from_ref, refs[5], refs[6])
            exchange_start(*small)

        sends = []

        def source(j, spot, part, own):
            if own:
                return ins[j].at[pl.ds(part * piece, piece)]
            return outs[j].at[window(spot, core, part)]

        def ring_copy(j, way, part, hop):
            spot = place - (hop - 1) * (1 - 2 * way)
            return pltpu.make_async_remote_copy(
                src_ref=source(j, spot, part, hop == 1),
                dst_ref=outs[j].at[window(spot, core, part)],
                send_sem=ring_send.at[j, way, part, hop - 1],
                recv_sem=ring_recv.at[j, way, part, hop - 1],
                device_id={"dp": neighbours[way]},
                device_id_type=pl.DeviceIdType.MESH,
            )

        def ring_arrival(j, way, part, hop):
            spot = place - hop * (1 - 2 * way)
            here = outs[j].at[window(spot, core, part)]
            return pltpu.make_async_remote_copy(
                src_ref=here,
                dst_ref=here,
                send_sem=ring_send.at[j, way, part, hop - 1],
                recv_sem=ring_recv.at[j, way, part, hop - 1],
                device_id={"dp": neighbours[way]},
                device_id_type=pl.DeviceIdType.MESH,
            )

        def side_copy(j, part, slot, spot, own):
            return pltpu.make_async_remote_copy(
                src_ref=source(j, spot, part, own),
                dst_ref=outs[j].at[window(spot, core, part)],
                send_sem=side_send.at[j, part, slot],
                recv_sem=side_recv.at[j, part, slot],
                device_id={"dp": partner},
                device_id_type=pl.DeviceIdType.MESH,
            )

        def side_arrival(j, part, slot, spot):
            here = outs[j].at[window(spot, 1 - core, part)]
            return pltpu.make_async_remote_copy(
                src_ref=here,
                dst_ref=here,
                send_sem=side_send.at[j, part, slot],
                recv_sem=side_recv.at[j, part, slot],
                device_id={"dp": partner},
                device_id_type=pl.DeviceIdType.MESH,
            )

        def launch(copy):
            copy.start()
            sends.append(copy)

        for part in range(parts):
            for j in range(count):
                for way in range(2):
                    launch(ring_copy(j, way, part, 1))
        owns = []
        for part in range(parts):
            for j in range(count):
                launch(side_copy(j, part, 0, place, True))
                own = pltpu.make_async_copy(
                    source(j, place, part, True),
                    outs[j].at[window(place, core, part)],
                    own_sem.at[j, part],
                )
                own.start()
                owns.append(own)
        if first is not None:
            exchange_finish(*small)
            values = rows_ref[...].astype(jnp.float32)
            normed, _ = norm_stats(values, EPSILON)
            mp_size = lax.axis_size("mp")
            for d in range(devices):
                cols = slice(d * rows, (d + 1) * rows)
                sent = from_ref[d * mp_size]
                norm_ref[0, :, cols] = (normed[:, cols] * sent[0:1] + sent[1:2]).astype(
                    norm_ref.dtype
                )
        for hop in range(1, half + 1):
            if first is not None and hop == 2:
                across = pltpu.make_async_remote_copy(
                    src_ref=norm_ref.at[0],
                    dst_ref=norm_ref.at[1],
                    send_sem=refs[7].at[0],
                    recv_sem=refs[7].at[1],
                    device_id={"mp": 1 - lax.axis_index("mp")},
                    device_id_type=pl.DeviceIdType.MESH,
                )
                across.start()
            for part in range(parts):
                for j in range(count):
                    for way in range(2):
                        if hop <= hops[way][part]:
                            ring_arrival(j, way, part, hop).wait_recv()
                            if hop < hops[way][part]:
                                launch(ring_copy(j, way, part, hop + 1))
                            turn = 1 - 2 * way
                            slot = (chips - hop * turn) % chips
                            launch(side_copy(j, part, slot, place - hop * turn, False))
        for own in owns:
            own.wait()
        for copy in sends:
            copy.wait_send()
        for slot in range(chips):
            for part in range(parts):
                for j in range(count):
                    side_arrival(j, part, slot, place + slot).wait_recv()
        if first is not None:
            across.wait()

    total = sum(shard.shape[1] for shard in shards) * rows * 2
    out_shape = [
        jax.ShapeDtypeStruct((devices * rows, shard.shape[1]), shard.dtype) for shard in shards
    ]
    in_specs = [pl.BlockSpec(memory_space=pl.ANY)] * count
    out_specs = [pl.BlockSpec(memory_space=pl.ANY)] * count
    scratch = [
        pltpu.SemaphoreType.DMA((count, parts)),
        pltpu.SemaphoreType.DMA((count, parts, chips)),
        pltpu.SemaphoreType.DMA((count, parts, chips)),
        pltpu.SemaphoreType.DMA((count, 2, parts, half)),
        pltpu.SemaphoreType.DMA((count, 2, parts, half)),
    ]
    extra = ()
    if first is not None:
        extra = first
        peers = devices * lax.axis_size("mp")
        in_specs = in_specs + [pl.BlockSpec(memory_space=pltpu.VMEM)] * 2
        out_specs = out_specs + [pl.BlockSpec(memory_space=pltpu.VMEM)] * 2
        out_shape = out_shape + [
            jax.ShapeDtypeStruct((peers, *first[0].shape[1:]), first[0].dtype),
            jax.ShapeDtypeStruct((2, *first[1].shape), jnp.bfloat16),
        ]
        scratch = scratch + [
            pltpu.SemaphoreType.DMA((peers,)),
            pltpu.SemaphoreType.DMA((peers,)),
            pltpu.SemaphoreType.DMA((2,)),
        ]
    return pl.pallas_call(
        kernel,
        out_shape=out_shape,
        in_specs=in_specs,
        out_specs=out_specs,
        scratch_shapes=scratch,
        compiler_params=pltpu.CompilerParams(collective_id=call_id, has_side_effects=True),
        cost_estimate=pl.CostEstimate(
            flops=0, bytes_accessed=total * devices * 4, transcendentals=0
        ),
    )(*shards, *extra)


def ring_total(rows):
    devices = lax.axis_size("dp")
    chips = devices // 2
    half = chips // 2
    hops = (half, chips - 1 - half)
    width = rows.shape[1]
    piece = rows.shape[0] // (2 * chips)
    low = rows.dtype

    def kernel(
        in_ref,
        out_ref,
        mate,
        mine,
        landed,
        packed,
        pair_sem,
        sum_send,
        sum_recv,
        ring_send,
        ring_recv,
        side_send,
        side_recv,
    ):
        index = lax.axis_index("dp")
        core, chip = index % 2, index // 2
        odd = chip % 2
        place = (1 - odd) * (chip // 2) + odd * (chips - 1 - chip // 2)

        def device_at(spot):
            spot = (spot + 2 * chips) % chips
            upper = spot // half
            there = (1 - upper) * (2 * spot) + upper * (2 * (chips - 1 - spot) + 1)
            return there * 2 + core

        def spot(k):
            return (place + k + 2 * chips) % chips

        partner = chip * 2 + 1 - core
        neighbours = (device_at(place + 1), device_at(place - 1))

        def copy_to(target, source, dest, send, recv):
            return pltpu.make_async_remote_copy(
                src_ref=source,
                dst_ref=dest,
                send_sem=send,
                recv_sem=recv,
                device_id={"dp": target},
                device_id_type=pl.DeviceIdType.MESH,
            )

        barrier = pltpu.get_barrier_semaphore()
        for target in (*neighbours, partner):
            pl.semaphore_signal(
                barrier, inc=1, device_id={"dp": target}, device_id_type=pl.DeviceIdType.MESH
            )
        pl.semaphore_wait(barrier, 3)

        pair = copy_to(partner, in_ref.at[1 - core], mate, pair_sem.at[0], pair_sem.at[1])
        pair.start()
        pair.wait()

        def add_mate(k, carry):
            mine[k] = (in_ref[core, k].astype(jnp.float32) + mate[k].astype(jnp.float32)).astype(
                low
            )
            return carry

        lax.fori_loop(0, chips, add_mate, 0)

        sends = []

        def launch(copy):
            copy.start()
            sends.append(copy)

        def sum_copy(way, step, source):
            return copy_to(
                neighbours[way],
                source,
                landed.at[way, step],
                sum_send.at[way, step],
                sum_recv.at[way, step],
            )

        for way in range(2):
            launch(sum_copy(way, 0, mine.at[spot(hops[way] * (1 - 2 * way))]))
        for step in range(1, half + 1):
            for way in range(2):
                if step <= hops[way]:
                    sum_copy(way, step - 1, landed.at[way, step - 1]).wait_recv()
                    if step < hops[way]:
                        ahead = spot((hops[way] - step) * (1 - 2 * way))
                        packed[way, step] = (
                            landed[way, step - 1].astype(jnp.float32)
                            + mine[ahead].astype(jnp.float32)
                        ).astype(low)
                        launch(sum_copy(way, step, packed.at[way, step]))
        out_ref[core, place] = (
            mine[place].astype(jnp.float32)
            + landed[0, hops[0] - 1].astype(jnp.float32)
            + landed[1, hops[1] - 1].astype(jnp.float32)
        ).astype(low)

        def ring_copy(way, hop):
            there = out_ref.at[core, spot(-(hop - 1) * (1 - 2 * way))]
            return copy_to(
                neighbours[way], there, there, ring_send.at[way, hop - 1], ring_recv.at[way, hop - 1]
            )

        def ring_arrival(way, hop):
            here = out_ref.at[core, spot(-hop * (1 - 2 * way))]
            return copy_to(
                neighbours[way], here, here, ring_send.at[way, hop - 1], ring_recv.at[way, hop - 1]
            )

        def side_copy(slot, which):
            there = out_ref.at[which, spot(slot)]
            return copy_to(partner, there, there, side_send.at[slot], side_recv.at[slot])

        for way in range(2):
            launch(ring_copy(way, 1))
        launch(side_copy(0, core))
        for hop in range(1, half + 1):
            for way in range(2):
                if hop <= hops[way]:
                    ring_arrival(way, hop).wait_recv()
                    if hop < hops[way]:
                        launch(ring_copy(way, hop + 1))
                    launch(side_copy((chips - hop * (1 - 2 * way)) % chips, core))
        for copy in sends:
            copy.wait_send()
        for slot in range(chips):
            side_copy(slot, 1 - core).wait_recv()

    shape = (2, chips, piece, width)
    total = pl.pallas_call(
        kernel,
        out_shape=jax.ShapeDtypeStruct(shape, low),
        in_specs=[pl.BlockSpec(memory_space=pltpu.VMEM)],
        out_specs=pl.BlockSpec(memory_space=pltpu.VMEM),
        scratch_shapes=[
            pltpu.VMEM(shape[1:], low),
            pltpu.VMEM(shape[1:], low),
            pltpu.VMEM((2, half, piece, width), low),
            pltpu.VMEM((2, half, piece, width), low),
            pltpu.SemaphoreType.DMA((2,)),
            pltpu.SemaphoreType.DMA((2, half)),
            pltpu.SemaphoreType.DMA((2, half)),
            pltpu.SemaphoreType.DMA((2, half)),
            pltpu.SemaphoreType.DMA((2, half)),
            pltpu.SemaphoreType.DMA((chips,)),
            pltpu.SemaphoreType.DMA((chips,)),
        ],
        compiler_params=pltpu.CompilerParams(collective_id=5, has_side_effects=True),
    )(rows.reshape(shape))
    return total.reshape(rows.shape)


def each_peer(action):
    dp_size, mp_size = lax.axis_size("dp"), lax.axis_size("mp")
    me = lax.axis_index("dp") * mp_size + lax.axis_index("mp")
    for place in range(dp_size * mp_size):
        pl.when(me != place)(
            functools.partial(action, place, place // mp_size, place % mp_size)
        )


def exchange_start(in_ref, out_ref, send_sem, recv_sem):
    dp_size, mp_size = lax.axis_size("dp"), lax.axis_size("mp")
    dp_index = lax.axis_index("dp")
    me = dp_index * mp_size + lax.axis_index("mp")
    barrier = pltpu.get_barrier_semaphore()

    def greet(place, row, col):
        pl.semaphore_signal(
            barrier, inc=1, device_id=(row, col), device_id_type=pl.DeviceIdType.MESH
        )

    each_peer(greet)
    pl.semaphore_wait(barrier, dp_size * mp_size - 1)

    def send(place, row, col):
        pltpu.make_async_remote_copy(
            src_ref=in_ref.at[row],
            dst_ref=out_ref.at[me],
            send_sem=send_sem.at[place],
            recv_sem=recv_sem.at[me],
            device_id=(row, col),
            device_id_type=pl.DeviceIdType.MESH,
        ).start()

    each_peer(send)
    out_ref[me] = in_ref[dp_index]


def exchange_finish(in_ref, out_ref, send_sem, recv_sem):
    def finish(place, row, col):
        copy = pltpu.make_async_remote_copy(
            src_ref=in_ref.at[row],
            dst_ref=out_ref.at[place],
            send_sem=send_sem.at[place],
            recv_sem=recv_sem.at[place],
            device_id=(row, col),
            device_id_type=pl.DeviceIdType.MESH,
        )
        copy.wait_send()
        copy.wait_recv()

    each_peer(finish)


def exchange_blocks(blocks):
    dp_size, mp_size = lax.axis_size("dp"), lax.axis_size("mp")
    total = dp_size * mp_size

    def kernel(in_ref, out_ref, send_sem, recv_sem):
        exchange_start(in_ref, out_ref, send_sem, recv_sem)
        exchange_finish(in_ref, out_ref, send_sem, recv_sem)

    return pl.pallas_call(
        kernel,
        out_shape=jax.ShapeDtypeStruct((total, *blocks.shape[1:]), blocks.dtype),
        in_specs=[pl.BlockSpec(memory_space=pltpu.VMEM)],
        out_specs=pl.BlockSpec(memory_space=pltpu.VMEM),
        scratch_shapes=[
            pltpu.SemaphoreType.DMA((total,)),
            pltpu.SemaphoreType.DMA((total,)),
        ],
        compiler_params=pltpu.CompilerParams(collective_id=2, has_side_effects=True),
    )(blocks)


def move_blocks(rows, table, outward):
    blocks = table.shape[0]
    width = rows.shape[1] // blocks

    def kernel(table_ref, in_ref, out_ref):
        for place in range(blocks):
            there = pl.ds(pl.multiple_of(table_ref[place] * width, width), width)
            here = pl.ds(place * width, width)
            if outward:
                out_ref[:, there] = in_ref[:, here]
            else:
                out_ref[:, here] = in_ref[:, there]

    if width % 128:
        order = table
        if outward:
            order = jnp.sum(
                jnp.where(table[None, :] == jnp.arange(blocks)[:, None], jnp.arange(blocks), 0),
                axis=1,
            )
        return jnp.take(rows.reshape(rows.shape[0], blocks, width), order, axis=1).reshape(
            rows.shape
        )
    return pl.pallas_call(
        kernel,
        out_shape=jax.ShapeDtypeStruct(rows.shape, rows.dtype),
        in_specs=[
            pl.BlockSpec(memory_space=pltpu.SMEM),
            pl.BlockSpec(memory_space=pltpu.VMEM),
        ],
        out_specs=pl.BlockSpec(memory_space=pltpu.VMEM),
    )(table, rows)


def swap_mp(rows):
    return lax.ppermute(rows, "mp", [(0, 1), (1, 0)])


def gather_rows(rows_low):
    return jnp.concatenate([rows_low, swap_mp(rows_low)], axis=0)


def scatter_rows(terms):
    half_rows = terms.shape[0] // 2
    arrived = swap_mp(terms[half_rows:].astype(jnp.bfloat16))
    return terms[:half_rows] + arrived.astype(jnp.float32)


def scatter_product(rows, weight):
    half_rows = rows.shape[0] // 2
    far = contract_last(rows[half_rows:], weight).astype(jnp.bfloat16)
    near = contract_last(tie(rows, far)[:half_rows], weight)
    return near + swap_mp(far).astype(jnp.float32)


def tie(value, other):
    return lax.optimization_barrier((value, other))[0]


def on_device(
    tokens_in,
    teacher,
    valid_mask,
    group_of,
    prompt_len,
    ln1_gain,
    ln1_bias,
    w_query,
    w_key,
    w_value,
    w_gate,
    w_out,
    ln2_gain,
    ln2_bias,
    w_up,
    w_down,
):
    half_rows = tokens_in.shape[0]
    model_dim = tokens_in.shape[1]
    seg_len = half_rows * lax.axis_size("mp")
    seg_count = group_of.shape[0]
    group_count = prompt_len.shape[0]
    heads_local = w_query.shape[1] // DK
    token_total = seg_len * seg_count
    dp_index = lax.axis_index("dp")
    mp_index = lax.axis_index("mp")
    ring = Ring()
    own_width = model_dim // 2
    table = ring.block_table()

    segment_ids = jnp.arange(seg_count, dtype=jnp.int32)
    my_group = jnp.sum(jnp.where(segment_ids == dp_index, group_of, 0))
    first_member = jnp.min(jnp.where(group_of == my_group, segment_ids, seg_count))
    prompt_flag = (first_member == dp_index).astype(jnp.float32)
    group_match = jnp.arange(group_count, dtype=jnp.int32) == my_group
    group_onehot = group_match.astype(jnp.float32)
    prompt_size = jnp.sum(jnp.where(group_match, prompt_len, 0))
    own_ids = mp_index * half_rows + jnp.arange(half_rows, dtype=jnp.int32)
    other_ids = (1 - mp_index) * half_rows + jnp.arange(half_rows, dtype=jnp.int32)
    token_ids = jnp.concatenate([own_ids, other_ids])
    loss_mask = valid_mask[0].astype(jnp.float32) * jnp.where(
        prompt_flag > 0, own_ids < prompt_size, True
    ).astype(jnp.float32)
    block = model_dim // ring.devices

    def packed(rows, scalar):
        split = rows.reshape(rows.shape[0], -1, block).transpose(1, 0, 2)
        split = jnp.pad(split, ((0, 0), (0, 0), (0, 128 - block)))
        extra = jnp.broadcast_to(scalar, (split.shape[0], 8 - rows.shape[0], 128))
        return jnp.concatenate([split, extra], axis=1)

    vectors = jnp.stack([ln1_gain, ln1_bias, ln2_gain, ln2_bias]).astype(jnp.float32)
    ones_own = jnp.sum(valid_mask).astype(jnp.float32)
    blocks_own = packed(jnp.tile(vectors, (1, ring.devices)), ones_own)
    inside = block == 128
    if inside:
        wk_full, wv_full, from_all, a_pair = gather_ring(
            [w_key, w_value], 1, (blocks_own, tokens_in)
        )
        a_all = a_pair.reshape(seg_len, model_dim)
    else:
        from_all = exchange_blocks(blocks_own)
    ones = jnp.sum(from_all[:, 4, 0].reshape(ring.devices, -1), axis=1)
    same_group = group_of[:, None] == group_of[None, :]
    firsts = jnp.min(jnp.where(same_group, segment_ids[None, :], seg_count), axis=1)
    group_ids = jnp.arange(group_count, dtype=jnp.int32)
    sizes = jnp.sum(
        jnp.where(group_of[:, None] == group_ids[None, :], prompt_len[None, :], 0), axis=1
    ).astype(jnp.float32)
    valid_count = jnp.sum(jnp.where(firsts == segment_ids, jnp.minimum(ones, sizes), ones))
    by_row = from_all.reshape(ring.devices, -1, 8, 128)[:, 0, :4, :block]
    gain_one, bias_one, gain_two, bias_two = (
        by_row[:, i].reshape(1, model_dim) for i in range(4)
    )

    def gather_all(shard):
        return lax.all_gather(shard, "dp", axis=0, tiled=True)

    offset = jnp.where(prompt_flag > 0, 0, prompt_size)
    positions = (token_ids + offset).astype(jnp.float32)
    head_ids = (mp_index * heads_local + jnp.arange(heads_local, dtype=jnp.int32)).astype(
        jnp.float32
    )
    log_decay = jnp.log(1.0 - 2.0 ** (-5.0 - head_ids))
    before_end = token_ids < prompt_size
    state_age = (prompt_size - 1 - token_ids).astype(jnp.float32)
    state_weighting = jnp.where(
        (before_end & (prompt_flag > 0))[:, None],
        jnp.exp(log_decay[None, :] * jnp.maximum(state_age, 0.0)[:, None]),
        0.0,
    )
    float_ids = token_ids.astype(jnp.float32)
    continuation_factor = (1.0 - prompt_flag) * jnp.exp(
        log_decay[None, :] * (float_ids + 1.0)[:, None]
    )
    distance = float_ids[:, None] - float_ids[None, :]
    decay_mat = jnp.where(
        distance[None] >= 0.0,
        jnp.exp(log_decay[:, None, None] * jnp.maximum(distance, 0.0)[None]),
        0.0,
    )
    token_rows = tokens_in.astype(jnp.float32)
    teacher_rows = teacher.astype(jnp.float32)
    normed_one, inv_one = norm_stats(token_rows, EPSILON)
    if not inside:
        a_all = gather_rows((normed_one * gain_one + bias_one).astype(jnp.bfloat16))
        wk_full, wv_full = gather_ring([w_key, w_value])
    keys_raw = lax.optimization_barrier(plain_dot(a_all, wk_full)).reshape(seg_len, heads_local, DK)
    reduced_values = (
        plain_dot(a_all, wv_full).astype(jnp.bfloat16).reshape(seg_len, heads_local, DV)
    )
    cosine, sine_tab, grow_fac = xpos_tables(positions, 1.0)
    _, _, shrink = xpos_tables(positions, -1.0)
    q_scale = DK ** (-0.5)
    rotated_keys = rotate_pairs(keys_raw, cosine, sine_tab, shrink).astype(jnp.bfloat16)
    local_state = jnp.einsum(
        "jld,jla->lda",
        (rotated_keys.astype(jnp.float32) * state_weighting[:, :, None]).astype(jnp.bfloat16),
        reduced_values,
        preferred_element_type=jnp.float32,
    )
    slots = (group_onehot[:, None, None, None] * (prompt_flag * local_state)[None]).astype(
        jnp.bfloat16
    )
    summed = lax.psum(slots, "dp")
    wq_full, wg_full, wo_full = gather_ring([tie(w_query, slots), w_gate, w_out], 3)
    wd_full = gather_all(tie(w_down, (wq_full, summed)))
    state_lookup = jnp.sum(
        summed.astype(jnp.float32) * group_onehot[:, None, None, None], axis=0
    ).astype(jnp.bfloat16)
    queries = lax.optimization_barrier(plain_dot(a_all, wq_full)).reshape(seg_len, heads_local, DK)
    gate_pre = lax.optimization_barrier(plain_dot(a_all, wg_full))
    rotated_queries = (rotate_pairs(queries, cosine, sine_tab, grow_fac) * q_scale).astype(
        jnp.bfloat16
    )
    scores = jnp.einsum(
        "thk,nhk->htn", rotated_queries, rotated_keys, preferred_element_type=jnp.float32
    )
    weights_low = (scores * decay_mat).astype(jnp.bfloat16)
    retained_output = jnp.einsum(
        "htn,nhv->thv", weights_low, reduced_values, preferred_element_type=jnp.float32
    )
    carried_forward = jnp.einsum(
        "ozi,ziw->ozw", rotated_queries, state_lookup, preferred_element_type=jnp.float32
    )
    retained_output = retained_output + continuation_factor[:, :, None] * carried_forward
    grouped, inv_group = norm_stats(retained_output, GROUP_EPSILON)
    gate_act = jax.nn.silu(gate_pre).reshape(seg_len, heads_local, DV)
    gated_out = (gate_act * grouped).reshape(seg_len, heads_local * DV).astype(jnp.bfloat16)
    attn_own = scatter_product(gated_out, wo_full)
    hidden_res = token_rows + attn_own
    normed_two, inv_two = norm_stats(hidden_res, EPSILON)
    c_own = (normed_two * gain_two + bias_two).astype(jnp.bfloat16)
    c_all = gather_rows(c_own)
    (wu_full,) = gather_ring([tie(w_up, c_own)], 4)
    up_pre = plain_dot(c_all, wu_full)
    up_act = jax.nn.gelu(up_pre, approximate=False).astype(jnp.bfloat16)
    ffn_own = scatter_product(up_act, wd_full)
    block_out = hidden_res + ffn_own
    error_rows = block_out - teacher_rows
    weighted = loss_mask[:, None] * error_rows
    squared_own = jnp.sum(weighted * error_rows)
    grad_out = token_total / valid_count * weighted

    def weight_grad(feature_side, other_side, flip):
        keep = contract_first(feature_side[:, :own_width], other_side).astype(jnp.bfloat16)
        give = contract_first(feature_side[:, own_width:], other_side).astype(jnp.bfloat16)
        return RingSum(ring, keep, ring.swap(give), flip)

    def in_order(rows):
        return move_blocks(rows, table, False)

    def then(value, *ring_sums):
        return tie(value, tuple(r.moving[way] for r in ring_sums for way in range(2)))

    grad_ffn_all = gather_rows(grad_out.astype(jnp.bfloat16))
    sum_wd = weight_grad(in_order(grad_ffn_all), up_act, False)
    grad_up_act = plain_dot(tie(grad_ffn_all, sum_wd.full), wd_full)
    _, gelu_pull = jax.vjp(lambda inner: jax.nn.gelu(inner, approximate=False), up_pre)
    grad_up = gelu_pull(grad_up_act)[0].astype(jnp.bfloat16)
    sum_wu = weight_grad(in_order(c_all), grad_up, True)
    sum_wd.run(1)
    grad_up = tie(then(grad_up, sum_wd), sum_wu.full)
    grad_c_parts = contract_last(grad_up, wu_full)
    grad_c = scatter_rows(grad_c_parts)
    sum_wd.run(1)
    grad_c = then(grad_c, sum_wd)
    grad_gain2_part = jnp.sum(grad_c * normed_two, axis=0)
    grad_bias2_part = jnp.sum(grad_c, axis=0)
    grad_hidden = grad_out + norm_back(grad_c * gain_two, normed_two, inv_two)
    grad_attn_all = gather_rows(grad_hidden.astype(jnp.bfloat16))
    sum_wd.run(2)
    sum_wu.run(1)
    grad_attn_all = then(grad_attn_all, sum_wd, sum_wu)
    sum_wo = weight_grad(in_order(grad_attn_all), gated_out, False)
    grad_attn_all = tie(grad_attn_all, sum_wo.full)
    grad_gated = plain_dot(grad_attn_all, wo_full).reshape(seg_len, heads_local, DV)
    _, silu_pull = jax.vjp(jax.nn.silu, gate_pre)
    grad_gate = silu_pull((grad_gated * grouped).reshape(seg_len, heads_local * DV))[0].astype(
        jnp.bfloat16
    )
    retained_gradient = norm_back(grad_gated * gate_act, grouped, inv_group).astype(jnp.bfloat16)
    state_grad_own = jnp.einsum(
        "ybn,ybw->bnw",
        (rotated_queries.astype(jnp.float32) * continuation_factor[:, :, None]).astype(
            jnp.bfloat16
        ),
        retained_gradient,
        preferred_element_type=jnp.float32,
    )
    grad_slots = (group_onehot[:, None, None, None] * state_grad_own[None]).astype(jnp.bfloat16)
    grad_summed = ring_total(grad_slots.reshape(-1, DV)).reshape(grad_slots.shape)
    retained_gradient = tie(retained_gradient, grad_summed)
    sum_wu.run(2)
    a_order = in_order(a_all)
    grad_gate = then(grad_gate, sum_wu)
    sum_wg = weight_grad(a_order, grad_gate, True)
    retained_gradient = tie(retained_gradient, sum_wg.full)
    sum_wu.run(1)
    sum_wo.run(1)
    grad_weights = jnp.einsum(
        "thv,nhv->htn", retained_gradient, reduced_values, preferred_element_type=jnp.float32
    )
    grad_values = jnp.einsum(
        "htn,thv->nhv", weights_low, retained_gradient, preferred_element_type=jnp.float32
    )
    grad_scores = then((grad_weights * decay_mat).astype(jnp.bfloat16), sum_wu, sum_wo)
    sum_wo.run(1)
    grad_q_rot = jnp.einsum(
        "htn,nhk->thk", grad_scores, rotated_keys, preferred_element_type=jnp.float32
    )
    grad_q_rot = grad_q_rot + continuation_factor[:, :, None] * jnp.einsum(
        "mjr,jwr->mjw", retained_gradient, state_lookup, preferred_element_type=jnp.float32
    )
    grad_k_rot = jnp.einsum(
        "htn,thk->nhk", grad_scores, rotated_queries, preferred_element_type=jnp.float32
    )
    grad_queries = (
        rotate_back(grad_q_rot * q_scale, cosine, sine_tab, grow_fac)
        .reshape(seg_len, heads_local * DK)
        .astype(jnp.bfloat16)
    )
    grad_queries = then(grad_queries, sum_wo)
    sum_wq = weight_grad(a_order, grad_queries, False)
    state_gradient = (
        prompt_flag
        * jnp.sum(grad_summed.astype(jnp.float32) * group_onehot[:, None, None, None], axis=0)
    ).astype(jnp.bfloat16)
    grad_k_rot = grad_k_rot + state_weighting[:, :, None] * jnp.einsum(
        "ilm,lpm->ilp", reduced_values, state_gradient, preferred_element_type=jnp.float32
    )
    grad_values = grad_values + state_weighting[:, :, None] * jnp.einsum(
        "zdo,doi->zdi", rotated_keys, state_gradient, preferred_element_type=jnp.float32
    )
    grad_keys = (
        rotate_back(grad_k_rot, cosine, sine_tab, shrink)
        .reshape(seg_len, heads_local * DK)
        .astype(jnp.bfloat16)
    )
    grad_vlow = grad_values.reshape(seg_len, heads_local * DV).astype(jnp.bfloat16)
    grad_key_value = jnp.concatenate([grad_keys, grad_vlow], axis=1)
    sum_wkv = weight_grad(a_order, grad_key_value, True)
    grad_keys = tie(grad_keys, sum_wkv.arrived)
    grad_a = scatter_rows(
        contract_last(grad_queries, wq_full)
        + contract_last(grad_gate, wg_full)
        + contract_last(grad_keys, wk_full)
        + contract_last(grad_vlow, wv_full)
    )
    sum_wo.run(2)
    sum_wg.run(1)
    grad_gain1_part = jnp.sum(grad_a * normed_one, axis=0)
    grad_bias1_part = jnp.sum(grad_a, axis=0)
    grad_tokens = grad_hidden + norm_back(grad_a * gain_one, normed_one, inv_one)

    sums = jnp.stack([grad_gain1_part, grad_bias1_part, grad_gain2_part, grad_bias2_part])
    totals = jnp.sum(exchange_blocks(packed(sums, squared_own)), axis=0)
    loss_value = totals[4, 0] / (valid_count * model_dim)
    key_width = w_key.shape[1]
    sum_wg.run(2)
    sum_wg.moving = [tie(x, totals) for x in sum_wg.moving]
    grad_wkv = sum_wkv.result()

    return (
        block_out,
        grad_tokens,
        loss_value,
        totals[0, :block],
        totals[1, :block],
        sum_wq.result(),
        grad_wkv[:, :key_width],
        grad_wkv[:, key_width:],
        sum_wg.result(),
        sum_wo.result(),
        totals[2, :block],
        totals[3, :block],
        sum_wu.result(),
        sum_wd.result(),
    )


def solution(mesh):
    return jax.shard_map(
        on_device,
        mesh=mesh,
        in_specs=(
            P(("dp", "mp"), None),
            P(("dp", "mp"), None),
            P("dp", "mp"),
            P(),
            P(),
            P("dp"),
            P("dp"),
            P("dp", "mp"),
            P("dp", "mp"),
            P("dp", "mp"),
            P("dp", "mp"),
            P("dp", "mp"),
            P("dp"),
            P("dp"),
            P("dp", "mp"),
            P("dp", "mp"),
        ),
        out_specs=(
            P(("dp", "mp"), None),
            P(("dp", "mp"), None),
            P(),
            P("dp"),
            P("dp"),
            P("dp", "mp"),
            P("dp", "mp"),
            P("dp", "mp"),
            P("dp", "mp"),
            P("dp", "mp"),
            P("dp"),
            P("dp"),
            P("dp", "mp"),
            P("dp", "mp"),
        ),
        check_vma=False,
    )
```

```python
import functools
import math

import jax
import jax.numpy as jnp
from jax import lax
from jax.experimental import pallas as pl
from jax.experimental.pallas import tpu as pltpu
from jax.sharding import PartitionSpec as P

DK = 256
DV = 512


EPSILON = 1e-05
GROUP_EPSILON = 0.05


def norm_stats(values, floor_eps):
    center = jnp.mean(values, axis=-1, keepdims=True)
    shifted = values - center
    inv_std = lax.rsqrt(jnp.mean(shifted * shifted, axis=-1, keepdims=True) + floor_eps)
    return (shifted * inv_std, inv_std)


def norm_back(grad_in, normed, inv_std):
    mean_grad = jnp.mean(grad_in, axis=-1, keepdims=True)
    mean_proj = jnp.mean(grad_in * normed, axis=-1, keepdims=True)
    return (grad_in - mean_grad - normed * mean_proj) * inv_std


def xpos_tables(positions, direction):
    half_dim = DK // 2
    pair_index = jnp.arange(half_dim, dtype=jnp.float32)
    frequency = jnp.exp(-(2.0 * pair_index / DK) * math.log(10000.0))
    base_ratio = (2.0 * pair_index / DK + 0.4) / 1.4
    angles = positions[:, None] * frequency[None, :]
    factor = jnp.exp(direction * (positions[:, None] / 512.0) * jnp.log(base_ratio)[None, :])
    return (jnp.cos(angles), jnp.sin(angles), factor)


def rotate_pairs(values, cosine, sine_tab, factor):
    half_dim = values.shape[-1] // 2
    first_half = values[..., :half_dim]
    second = values[..., half_dim:]
    cosine = cosine[:, None, :]
    sine_tab = sine_tab[:, None, :]
    factor = factor[:, None, :]
    return jnp.concatenate(
        [
            (first_half * cosine - second * sine_tab) * factor,
            (second * cosine + first_half * sine_tab) * factor,
        ],
        axis=-1,
    )


def rotate_back(grad_rot, cosine, sine_tab, factor):
    half_dim = grad_rot.shape[-1] // 2
    first_half = grad_rot[..., :half_dim]
    second = grad_rot[..., half_dim:]
    cosine = cosine[:, None, :]
    sine_tab = sine_tab[:, None, :]
    factor = factor[:, None, :]
    return jnp.concatenate(
        [
            (first_half * cosine + second * sine_tab) * factor,
            (second * cosine - first_half * sine_tab) * factor,
        ],
        axis=-1,
    )


def plain_dot(first_op, second_op):
    return jnp.dot(first_op, second_op, preferred_element_type=jnp.float32)


def contract_last(first_op, second_op):
    return lax.dot_general(
        first_op, second_op, (((1,), (1,)), ((), ())), preferred_element_type=jnp.float32
    )


def contract_first(first_op, second_op):
    return lax.dot_general(
        first_op, second_op, (((0,), (0,)), ((), ())), preferred_element_type=jnp.float32
    )


class Ring:
    def __init__(self):
        self.devices = lax.axis_size("dp")
        self.chips = self.devices // 2
        half = self.chips // 2
        self.order = [2 * a for a in range(half)] + [2 * a + 1 for a in reversed(range(half))]
        self.index = lax.axis_index("dp")
        self.core = self.index % 2
        chip = self.index // 2
        self.place = jnp.where(chip % 2 == 0, chip // 2, self.chips - 1 - chip // 2)
        self.near = self.chips // 2
        self.far = self.chips - 1 - self.near

    def shift(self, rows, step):
        pairs = [
            (self.order[i] * 2 + c, self.order[(i + step) % self.chips] * 2 + c)
            for i in range(self.chips)
            for c in range(2)
        ]
        return lax.ppermute(rows, "dp", pairs)

    def swap(self, rows):
        return lax.ppermute(rows, "dp", [(i, i ^ 1) for i in range(self.devices)])

    def hops(self, flip):
        return (self.far, self.near) if flip else (self.near, self.far)

    def block_table(self):
        spot = (self.place + jnp.arange(self.chips, dtype=jnp.int32)) % self.chips
        chip = jnp.where(spot < self.chips // 2, 2 * spot, 2 * (self.chips - 1 - spot) + 1)
        return jnp.concatenate([chip * 2 + self.core, chip * 2 + 1 - self.core]).astype(jnp.int32)


class RingSum:
    def __init__(self, ring, full, arrived, flip):
        self.ring = ring
        self.full = full
        self.arrived = arrived
        self.block = full.shape[0] // ring.chips
        self.up, self.down = ring.hops(flip)
        self.moving = [
            self.term(k).astype(jnp.bfloat16) for k in (self.up, ring.chips - self.down)
        ]
        self.count = 0

    def term(self, k):
        rows = slice(k * self.block, (k + 1) * self.block)
        return self.full[rows].astype(jnp.float32) + self.arrived[rows].astype(jnp.float32)

    def step(self):
        ring = self.ring
        self.count += 1
        for way, hops, k in (
            (0, self.up, self.up - self.count),
            (1, self.down, ring.chips - self.down + self.count),
        ):
            if self.count <= hops:
                moved = ring.shift(self.moving[way], 1 - 2 * way)
                if self.count < hops:
                    moved = (moved.astype(jnp.float32) + self.term(k)).astype(jnp.bfloat16)
                self.moving[way] = moved

    def run(self, steps):
        for _ in range(min(steps, max(self.up, self.down) - self.count)):
            self.step()

    def result(self):
        self.run(self.ring.chips)
        return (
            self.term(0)
            + self.moving[0].astype(jnp.float32)
            + self.moving[1].astype(jnp.float32)
        )


def gather_ring(shards, call_id=1, first=None):
    devices = lax.axis_size("dp")
    chips = devices // 2
    half = chips // 2
    rows = shards[0].shape[0]
    count = len(shards)
    parts = 2
    piece = rows // parts
    hops = ((half, half - 1), (half - 1, half))

    def kernel(*refs):
        ins, refs = refs[:count], refs[count:]
        if first is not None:
            (blocks_ref, rows_ref), refs = refs[:2], refs[2:]
        outs, refs = refs[:count], refs[count:]
        if first is not None:
            (from_ref, norm_ref), refs = refs[:2], refs[2:]
        own_sem, side_send, side_recv, ring_send, ring_recv = refs[:5]
        index = lax.axis_index("dp")
        core, chip = index % 2, index // 2
        odd = chip % 2
        place = (1 - odd) * (chip // 2) + odd * (chips - 1 - chip // 2)

        def device_at(spot, which):
            spot = (spot + 2 * chips) % chips
            upper = spot // half
            there = (1 - upper) * (2 * spot) + upper * (2 * (chips - 1 - spot) + 1)
            return there * 2 + which

        def window(spot, which, part):
            first = device_at(spot, which) * rows + part * piece
            return pl.ds(pl.multiple_of(first, piece), piece)

        partner = chip * 2 + 1 - core
        neighbours = (device_at(place + 1, core), device_at(place - 1, core))

        if first is None:
            barrier = pltpu.get_barrier_semaphore()
            for target in (*neighbours, partner):
                pl.semaphore_signal(
                    barrier, inc=1, device_id={"dp": target}, device_id_type=pl.DeviceIdType.MESH
                )
            pl.semaphore_wait(barrier, 3)
        else:
            small = (blocks_ref, from_ref, refs[5], refs[6])
            exchange_start(*small)

        sends = []

        def source(j, spot, part, own):
            if own:
                return ins[j].at[pl.ds(part * piece, piece)]
            return outs[j].at[window(spot, core, part)]

        def ring_copy(j, way, part, hop):
            spot = place - (hop - 1) * (1 - 2 * way)
            return pltpu.make_async_remote_copy(
                src_ref=source(j, spot, part, hop == 1),
                dst_ref=outs[j].at[window(spot, core, part)],
                send_sem=ring_send.at[j, way, part, hop - 1],
                recv_sem=ring_recv.at[j, way, part, hop - 1],
                device_id={"dp": neighbours[way]},
                device_id_type=pl.DeviceIdType.MESH,
            )

        def ring_arrival(j, way, part, hop):
            spot = place - hop * (1 - 2 * way)
            here = outs[j].at[window(spot, core, part)]
            return pltpu.make_async_remote_copy(
                src_ref=here,
                dst_ref=here,
                send_sem=ring_send.at[j, way, part, hop - 1],
                recv_sem=ring_recv.at[j, way, part, hop - 1],
                device_id={"dp": neighbours[way]},
                device_id_type=pl.DeviceIdType.MESH,
            )

        def side_copy(j, part, slot, spot, own):
            return pltpu.make_async_remote_copy(
                src_ref=source(j, spot, part, own),
                dst_ref=outs[j].at[window(spot, core, part)],
                send_sem=side_send.at[j, part, slot],
                recv_sem=side_recv.at[j, part, slot],
                device_id={"dp": partner},
                device_id_type=pl.DeviceIdType.MESH,
            )

        def side_arrival(j, part, slot, spot):
            here = outs[j].at[window(spot, 1 - core, part)]
            return pltpu.make_async_remote_copy(
                src_ref=here,
                dst_ref=here,
                send_sem=side_send.at[j, part, slot],
                recv_sem=side_recv.at[j, part, slot],
                device_id={"dp": partner},
                device_id_type=pl.DeviceIdType.MESH,
            )

        def launch(copy):
            copy.start()
            sends.append(copy)

        for part in range(parts):
            for j in range(count):
                for way in range(2):
                    launch(ring_copy(j, way, part, 1))
        owns = []
        for part in range(parts):
            for j in range(count):
                launch(side_copy(j, part, 0, place, True))
                own = pltpu.make_async_copy(
                    source(j, place, part, True),
                    outs[j].at[window(place, core, part)],
                    own_sem.at[j, part],
                )
                own.start()
                owns.append(own)
        if first is not None:
            exchange_finish(*small)
            values = rows_ref[...].astype(jnp.float32)
            normed, _ = norm_stats(values, EPSILON)
            mp_size = lax.axis_size("mp")
            for d in range(devices):
                cols = slice(d * rows, (d + 1) * rows)
                sent = from_ref[d * mp_size]
                norm_ref[0, :, cols] = (normed[:, cols] * sent[0:1] + sent[1:2]).astype(
                    norm_ref.dtype
                )
        for hop in range(1, half + 1):
            if first is not None and hop == 2:
                across = pltpu.make_async_remote_copy(
                    src_ref=norm_ref.at[0],
                    dst_ref=norm_ref.at[1],
                    send_sem=refs[7].at[0],
                    recv_sem=refs[7].at[1],
                    device_id={"mp": 1 - lax.axis_index("mp")},
                    device_id_type=pl.DeviceIdType.MESH,
                )
                across.start()
            for part in range(parts):
                for j in range(count):
                    for way in range(2):
                        if hop <= hops[way][part]:
                            ring_arrival(j, way, part, hop).wait_recv()
                            if hop < hops[way][part]:
                                launch(ring_copy(j, way, part, hop + 1))
                            turn = 1 - 2 * way
                            slot = (chips - hop * turn) % chips
                            launch(side_copy(j, part, slot, place - hop * turn, False))
        for own in owns:
            own.wait()
        for copy in sends:
            copy.wait_send()
        for slot in range(chips):
            for part in range(parts):
                for j in range(count):
                    side_arrival(j, part, slot, place + slot).wait_recv()
        if first is not None:
            across.wait()

    total = sum(shard.shape[1] for shard in shards) * rows * 2
    out_shape = [
        jax.ShapeDtypeStruct((devices * rows, shard.shape[1]), shard.dtype) for shard in shards
    ]
    in_specs = [pl.BlockSpec(memory_space=pl.ANY)] * count
    out_specs = [pl.BlockSpec(memory_space=pl.ANY)] * count
    scratch = [
        pltpu.SemaphoreType.DMA((count, parts)),
        pltpu.SemaphoreType.DMA((count, parts, chips)),
        pltpu.SemaphoreType.DMA((count, parts, chips)),
        pltpu.SemaphoreType.DMA((count, 2, parts, half)),
        pltpu.SemaphoreType.DMA((count, 2, parts, half)),
    ]
    extra = ()
    if first is not None:
        extra = first
        peers = devices * lax.axis_size("mp")
        in_specs = in_specs + [pl.BlockSpec(memory_space=pltpu.VMEM)] * 2
        out_specs = out_specs + [pl.BlockSpec(memory_space=pltpu.VMEM)] * 2
        out_shape = out_shape + [
            jax.ShapeDtypeStruct((peers, *first[0].shape[1:]), first[0].dtype),
            jax.ShapeDtypeStruct((2, *first[1].shape), jnp.bfloat16),
        ]
        scratch = scratch + [
            pltpu.SemaphoreType.DMA((peers,)),
            pltpu.SemaphoreType.DMA((peers,)),
            pltpu.SemaphoreType.DMA((2,)),
        ]
    return pl.pallas_call(
        kernel,
        out_shape=out_shape,
        in_specs=in_specs,
        out_specs=out_specs,
        scratch_shapes=scratch,
        compiler_params=pltpu.CompilerParams(collective_id=call_id, has_side_effects=True),
        cost_estimate=pl.CostEstimate(
            flops=0, bytes_accessed=total * devices * 4, transcendentals=0
        ),
    )(*shards, *extra)


def ring_total(rows):
    devices = lax.axis_size("dp")
    chips = devices // 2
    half = chips // 2
    hops = (half, chips - 1 - half)
    width = rows.shape[1]
    piece = rows.shape[0] // (2 * chips)
    low = rows.dtype

    def kernel(
        in_ref,
        out_ref,
        mate,
        mine,
        landed,
        packed,
        pair_sem,
        sum_send,
        sum_recv,
        ring_send,
        ring_recv,
        side_send,
        side_recv,
    ):
        index = lax.axis_index("dp")
        core, chip = index % 2, index // 2
        odd = chip % 2
        place = (1 - odd) * (chip // 2) + odd * (chips - 1 - chip // 2)

        def device_at(spot):
            spot = (spot + 2 * chips) % chips
            upper = spot // half
            there = (1 - upper) * (2 * spot) + upper * (2 * (chips - 1 - spot) + 1)
            return there * 2 + core

        def spot(k):
            return (place + k + 2 * chips) % chips

        partner = chip * 2 + 1 - core
        neighbours = (device_at(place + 1), device_at(place - 1))

        def copy_to(target, source, dest, send, recv):
            return pltpu.make_async_remote_copy(
                src_ref=source,
                dst_ref=dest,
                send_sem=send,
                recv_sem=recv,
                device_id={"dp": target},
                device_id_type=pl.DeviceIdType.MESH,
            )

        barrier = pltpu.get_barrier_semaphore()
        for target in (*neighbours, partner):
            pl.semaphore_signal(
                barrier, inc=1, device_id={"dp": target}, device_id_type=pl.DeviceIdType.MESH
            )
        pl.semaphore_wait(barrier, 3)

        pair = copy_to(partner, in_ref.at[1 - core], mate, pair_sem.at[0], pair_sem.at[1])
        pair.start()
        pair.wait()

        def add_mate(k, carry):
            mine[k] = (in_ref[core, k].astype(jnp.float32) + mate[k].astype(jnp.float32)).astype(
                low
            )
            return carry

        lax.fori_loop(0, chips, add_mate, 0)

        sends = []

        def launch(copy):
            copy.start()
            sends.append(copy)

        def sum_copy(way, step, source):
            return copy_to(
                neighbours[way],
                source,
                landed.at[way, step],
                sum_send.at[way, step],
                sum_recv.at[way, step],
            )

        for way in range(2):
            launch(sum_copy(way, 0, mine.at[spot(hops[way] * (1 - 2 * way))]))
        for step in range(1, half + 1):
            for way in range(2):
                if step <= hops[way]:
                    sum_copy(way, step - 1, landed.at[way, step - 1]).wait_recv()
                    if step < hops[way]:
                        ahead = spot((hops[way] - step) * (1 - 2 * way))
                        packed[way, step] = (
                            landed[way, step - 1].astype(jnp.float32)
                            + mine[ahead].astype(jnp.float32)
                        ).astype(low)
                        launch(sum_copy(way, step, packed.at[way, step]))
        out_ref[core, place] = (
            mine[place].astype(jnp.float32)
            + landed[0, hops[0] - 1].astype(jnp.float32)
            + landed[1, hops[1] - 1].astype(jnp.float32)
        ).astype(low)

        def ring_copy(way, hop):
            there = out_ref.at[core, spot(-(hop - 1) * (1 - 2 * way))]
            return copy_to(
                neighbours[way], there, there, ring_send.at[way, hop - 1], ring_recv.at[way, hop - 1]
            )

        def ring_arrival(way, hop):
            here = out_ref.at[core, spot(-hop * (1 - 2 * way))]
            return copy_to(
                neighbours[way], here, here, ring_send.at[way, hop - 1], ring_recv.at[way, hop - 1]
            )

        def side_copy(slot, which):
            there = out_ref.at[which, spot(slot)]
            return copy_to(partner, there, there, side_send.at[slot], side_recv.at[slot])

        for way in range(2):
            launch(ring_copy(way, 1))
        launch(side_copy(0, core))
        for hop in range(1, half + 1):
            for way in range(2):
                if hop <= hops[way]:
                    ring_arrival(way, hop).wait_recv()
                    if hop < hops[way]:
                        launch(ring_copy(way, hop + 1))
                    launch(side_copy((chips - hop * (1 - 2 * way)) % chips, core))
        for copy in sends:
            copy.wait_send()
        for slot in range(chips):
            side_copy(slot, 1 - core).wait_recv()

    shape = (2, chips, piece, width)
    total = pl.pallas_call(
        kernel,
        out_shape=jax.ShapeDtypeStruct(shape, low),
        in_specs=[pl.BlockSpec(memory_space=pltpu.VMEM)],
        out_specs=pl.BlockSpec(memory_space=pltpu.VMEM),
        scratch_shapes=[
            pltpu.VMEM(shape[1:], low),
            pltpu.VMEM(shape[1:], low),
            pltpu.VMEM((2, half, piece, width), low),
            pltpu.VMEM((2, half, piece, width), low),
            pltpu.SemaphoreType.DMA((2,)),
            pltpu.SemaphoreType.DMA((2, half)),
            pltpu.SemaphoreType.DMA((2, half)),
            pltpu.SemaphoreType.DMA((2, half)),
            pltpu.SemaphoreType.DMA((2, half)),
            pltpu.SemaphoreType.DMA((chips,)),
            pltpu.SemaphoreType.DMA((chips,)),
        ],
        compiler_params=pltpu.CompilerParams(collective_id=5, has_side_effects=True),
    )(rows.reshape(shape))
    return total.reshape(rows.shape)


def each_peer(action):
    dp_size, mp_size = lax.axis_size("dp"), lax.axis_size("mp")
    me = lax.axis_index("dp") * mp_size + lax.axis_index("mp")
    for place in range(dp_size * mp_size):
        pl.when(me != place)(
            functools.partial(action, place, place // mp_size, place % mp_size)
        )


def exchange_start(in_ref, out_ref, send_sem, recv_sem):
    dp_size, mp_size = lax.axis_size("dp"), lax.axis_size("mp")
    dp_index = lax.axis_index("dp")
    me = dp_index * mp_size + lax.axis_index("mp")
    barrier = pltpu.get_barrier_semaphore()

    def greet(place, row, col):
        pl.semaphore_signal(
            barrier, inc=1, device_id=(row, col), device_id_type=pl.DeviceIdType.MESH
        )

    each_peer(greet)
    pl.semaphore_wait(barrier, dp_size * mp_size - 1)

    def send(place, row, col):
        pltpu.make_async_remote_copy(
            src_ref=in_ref.at[row],
            dst_ref=out_ref.at[me],
            send_sem=send_sem.at[place],
            recv_sem=recv_sem.at[me],
            device_id=(row, col),
            device_id_type=pl.DeviceIdType.MESH,
        ).start()

    each_peer(send)
    out_ref[me] = in_ref[dp_index]


def exchange_finish(in_ref, out_ref, send_sem, recv_sem):
    def finish(place, row, col):
        copy = pltpu.make_async_remote_copy(
            src_ref=in_ref.at[row],
            dst_ref=out_ref.at[place],
            send_sem=send_sem.at[place],
            recv_sem=recv_sem.at[place],
            device_id=(row, col),
            device_id_type=pl.DeviceIdType.MESH,
        )
        copy.wait_send()
        copy.wait_recv()

    each_peer(finish)


def exchange_blocks(blocks):
    dp_size, mp_size = lax.axis_size("dp"), lax.axis_size("mp")
    total = dp_size * mp_size

    def kernel(in_ref, out_ref, send_sem, recv_sem):
        exchange_start(in_ref, out_ref, send_sem, recv_sem)
        exchange_finish(in_ref, out_ref, send_sem, recv_sem)

    return pl.pallas_call(
        kernel,
        out_shape=jax.ShapeDtypeStruct((total, *blocks.shape[1:]), blocks.dtype),
        in_specs=[pl.BlockSpec(memory_space=pltpu.VMEM)],
        out_specs=pl.BlockSpec(memory_space=pltpu.VMEM),
        scratch_shapes=[
            pltpu.SemaphoreType.DMA((total,)),
            pltpu.SemaphoreType.DMA((total,)),
        ],
        compiler_params=pltpu.CompilerParams(collective_id=2, has_side_effects=True),
    )(blocks)


def move_blocks(rows, table, outward):
    blocks = table.shape[0]
    width = rows.shape[1] // blocks

    def kernel(table_ref, in_ref, out_ref):
        for place in range(blocks):
            there = pl.ds(pl.multiple_of(table_ref[place] * width, width), width)
            here = pl.ds(place * width, width)
            if outward:
                out_ref[:, there] = in_ref[:, here]
            else:
                out_ref[:, here] = in_ref[:, there]

    if width % 128:
        order = table
        if outward:
            order = jnp.sum(
                jnp.where(table[None, :] == jnp.arange(blocks)[:, None], jnp.arange(blocks), 0),
                axis=1,
            )
        return jnp.take(rows.reshape(rows.shape[0], blocks, width), order, axis=1).reshape(
            rows.shape
        )
    return pl.pallas_call(
        kernel,
        out_shape=jax.ShapeDtypeStruct(rows.shape, rows.dtype),
        in_specs=[
            pl.BlockSpec(memory_space=pltpu.SMEM),
            pl.BlockSpec(memory_space=pltpu.VMEM),
        ],
        out_specs=pl.BlockSpec(memory_space=pltpu.VMEM),
    )(table, rows)


def swap_mp(rows):
    return lax.ppermute(rows, "mp", [(0, 1), (1, 0)])


def gather_rows(rows_low):
    return jnp.concatenate([rows_low, swap_mp(rows_low)], axis=0)


def scatter_rows(terms):
    half_rows = terms.shape[0] // 2
    arrived = swap_mp(terms[half_rows:].astype(jnp.bfloat16))
    return terms[:half_rows] + arrived.astype(jnp.float32)


def scatter_product(rows, weight):
    half_rows = rows.shape[0] // 2
    far = contract_last(rows[half_rows:], weight).astype(jnp.bfloat16)
    near = contract_last(tie(rows, far)[:half_rows], weight)
    return near + swap_mp(far).astype(jnp.float32)


def tie(value, other):
    return lax.optimization_barrier((value, other))[0]


def on_device(
    tokens_in,
    teacher,
    valid_mask,
    group_of,
    prompt_len,
    ln1_gain,
    ln1_bias,
    w_query,
    w_key,
    w_value,
    w_gate,
    w_out,
    ln2_gain,
    ln2_bias,
    w_up,
    w_down,
):
    half_rows = tokens_in.shape[0]
    model_dim = tokens_in.shape[1]
    seg_len = half_rows * lax.axis_size("mp")
    seg_count = group_of.shape[0]
    group_count = prompt_len.shape[0]
    heads_local = w_query.shape[1] // DK
    token_total = seg_len * seg_count
    dp_index = lax.axis_index("dp")
    mp_index = lax.axis_index("mp")
    ring = Ring()
    own_width = model_dim // 2
    table = ring.block_table()

    segment_ids = jnp.arange(seg_count, dtype=jnp.int32)
    my_group = jnp.sum(jnp.where(segment_ids == dp_index, group_of, 0))
    first_member = jnp.min(jnp.where(group_of == my_group, segment_ids, seg_count))
    prompt_flag = (first_member == dp_index).astype(jnp.float32)
    group_match = jnp.arange(group_count, dtype=jnp.int32) == my_group
    group_onehot = group_match.astype(jnp.float32)
    prompt_size = jnp.sum(jnp.where(group_match, prompt_len, 0))
    own_ids = mp_index * half_rows + jnp.arange(half_rows, dtype=jnp.int32)
    other_ids = (1 - mp_index) * half_rows + jnp.arange(half_rows, dtype=jnp.int32)
    token_ids = jnp.concatenate([own_ids, other_ids])
    loss_mask = valid_mask[0].astype(jnp.float32) * jnp.where(
        prompt_flag > 0, own_ids < prompt_size, True
    ).astype(jnp.float32)
    block = model_dim // ring.devices

    def packed(rows, scalar):
        split = rows.reshape(rows.shape[0], -1, block).transpose(1, 0, 2)
        split = jnp.pad(split, ((0, 0), (0, 0), (0, 128 - block)))
        extra = jnp.broadcast_to(scalar, (split.shape[0], 8 - rows.shape[0], 128))
        return jnp.concatenate([split, extra], axis=1)

    vectors = jnp.stack([ln1_gain, ln1_bias, ln2_gain, ln2_bias]).astype(jnp.float32)
    ones_own = jnp.sum(valid_mask).astype(jnp.float32)
    blocks_own = packed(jnp.tile(vectors, (1, ring.devices)), ones_own)
    inside = block == 128
    if inside:
        wk_full, wv_full, from_all, a_pair = gather_ring(
            [w_key, w_value], 1, (blocks_own, tokens_in)
        )
        a_all = a_pair.reshape(seg_len, model_dim)
    else:
        from_all = exchange_blocks(blocks_own)
    ones = jnp.sum(from_all[:, 4, 0].reshape(ring.devices, -1), axis=1)
    same_group = group_of[:, None] == group_of[None, :]
    firsts = jnp.min(jnp.where(same_group, segment_ids[None, :], seg_count), axis=1)
    group_ids = jnp.arange(group_count, dtype=jnp.int32)
    sizes = jnp.sum(
        jnp.where(group_of[:, None] == group_ids[None, :], prompt_len[None, :], 0), axis=1
    ).astype(jnp.float32)
    valid_count = jnp.sum(jnp.where(firsts == segment_ids, jnp.minimum(ones, sizes), ones))
    by_row = from_all.reshape(ring.devices, -1, 8, 128)[:, 0, :4, :block]
    gain_one, bias_one, gain_two, bias_two = (
        by_row[:, i].reshape(1, model_dim) for i in range(4)
    )

    def gather_all(shard):
        return lax.all_gather(shard, "dp", axis=0, tiled=True)

    offset = jnp.where(prompt_flag > 0, 0, prompt_size)
    positions = (token_ids + offset).astype(jnp.float32)
    head_ids = (mp_index * heads_local + jnp.arange(heads_local, dtype=jnp.int32)).astype(
        jnp.float32
    )
    log_decay = jnp.log(1.0 - 2.0 ** (-5.0 - head_ids))
    before_end = token_ids < prompt_size
    state_age = (prompt_size - 1 - token_ids).astype(jnp.float32)
    state_weighting = jnp.where(
        (before_end & (prompt_flag > 0))[:, None],
        jnp.exp(log_decay[None, :] * jnp.maximum(state_age, 0.0)[:, None]),
        0.0,
    )
    float_ids = token_ids.astype(jnp.float32)
    continuation_factor = (1.0 - prompt_flag) * jnp.exp(
        log_decay[None, :] * (float_ids + 1.0)[:, None]
    )
    distance = float_ids[:, None] - float_ids[None, :]
    decay_mat = jnp.where(
        distance[None] >= 0.0,
        jnp.exp(log_decay[:, None, None] * jnp.maximum(distance, 0.0)[None]),
        0.0,
    )
    token_rows = tokens_in.astype(jnp.float32)
    teacher_rows = teacher.astype(jnp.float32)
    normed_one, inv_one = norm_stats(token_rows, EPSILON)
    if not inside:
        a_all = gather_rows((normed_one * gain_one + bias_one).astype(jnp.bfloat16))
        wk_full, wv_full = gather_ring([w_key, w_value])
    keys_raw = lax.optimization_barrier(plain_dot(a_all, wk_full)).reshape(seg_len, heads_local, DK)
    reduced_values = (
        plain_dot(a_all, wv_full).astype(jnp.bfloat16).reshape(seg_len, heads_local, DV)
    )
    cosine, sine_tab, grow_fac = xpos_tables(positions, 1.0)
    _, _, shrink = xpos_tables(positions, -1.0)
    q_scale = DK ** (-0.5)
    rotated_keys = rotate_pairs(keys_raw, cosine, sine_tab, shrink).astype(jnp.bfloat16)
    local_state = jnp.einsum(
        "jld,jla->lda",
        (rotated_keys.astype(jnp.float32) * state_weighting[:, :, None]).astype(jnp.bfloat16),
        reduced_values,
        preferred_element_type=jnp.float32,
    )
    slots = (group_onehot[:, None, None, None] * (prompt_flag * local_state)[None]).astype(
        jnp.bfloat16
    )
    summed = lax.psum(slots, "dp")
    wq_full, wg_full, wo_full = gather_ring([tie(w_query, slots), w_gate, w_out], 3)
    wd_full = gather_all(tie(w_down, (wq_full, summed)))
    state_lookup = jnp.sum(
        summed.astype(jnp.float32) * group_onehot[:, None, None, None], axis=0
    ).astype(jnp.bfloat16)
    queries = lax.optimization_barrier(plain_dot(a_all, wq_full)).reshape(seg_len, heads_local, DK)
    gate_pre = lax.optimization_barrier(plain_dot(a_all, wg_full))
    rotated_queries = (rotate_pairs(queries, cosine, sine_tab, grow_fac) * q_scale).astype(
        jnp.bfloat16
    )
    scores = jnp.einsum(
        "thk,nhk->htn", rotated_queries, rotated_keys, preferred_element_type=jnp.float32
    )
    weights_low = (scores * decay_mat).astype(jnp.bfloat16)
    retained_output = jnp.einsum(
        "htn,nhv->thv", weights_low, reduced_values, preferred_element_type=jnp.float32
    )
    carried_forward = jnp.einsum(
        "ozi,ziw->ozw", rotated_queries, state_lookup, preferred_element_type=jnp.float32
    )
    retained_output = retained_output + continuation_factor[:, :, None] * carried_forward
    grouped, inv_group = norm_stats(retained_output, GROUP_EPSILON)
    gate_act = jax.nn.silu(gate_pre).reshape(seg_len, heads_local, DV)
    gated_out = (gate_act * grouped).reshape(seg_len, heads_local * DV).astype(jnp.bfloat16)
    attn_own = scatter_product(gated_out, wo_full)
    hidden_res = token_rows + attn_own
    normed_two, inv_two = norm_stats(hidden_res, EPSILON)
    c_own = (normed_two * gain_two + bias_two).astype(jnp.bfloat16)
    c_all = gather_rows(c_own)
    (wu_full,) = gather_ring([tie(w_up, c_own)], 4)
    up_pre = plain_dot(c_all, wu_full)
    up_act = jax.nn.gelu(up_pre, approximate=False).astype(jnp.bfloat16)
    ffn_own = scatter_product(up_act, wd_full)
    block_out = hidden_res + ffn_own
    error_rows = block_out - teacher_rows
    weighted = loss_mask[:, None] * error_rows
    squared_own = jnp.sum(weighted * error_rows)
    grad_out = token_total / valid_count * weighted

    def weight_grad(feature_side, other_side, flip):
        keep = contract_first(feature_side[:, :own_width], other_side).astype(jnp.bfloat16)
        give = contract_first(feature_side[:, own_width:], other_side).astype(jnp.bfloat16)
        return RingSum(ring, keep, ring.swap(give), flip)

    def in_order(rows):
        return move_blocks(rows, table, False)

    def then(value, *ring_sums):
        return tie(value, tuple(r.moving[way] for r in ring_sums for way in range(2)))

    grad_ffn_all = gather_rows(grad_out.astype(jnp.bfloat16))
    sum_wd = weight_grad(in_order(grad_ffn_all), up_act, False)
    grad_up_act = plain_dot(tie(grad_ffn_all, sum_wd.full), wd_full)
    _, gelu_pull = jax.vjp(lambda inner: jax.nn.gelu(inner, approximate=False), up_pre)
    grad_up = gelu_pull(grad_up_act)[0].astype(jnp.bfloat16)
    sum_wu = weight_grad(in_order(c_all), grad_up, True)
    sum_wd.run(1)
    grad_up = tie(then(grad_up, sum_wd), sum_wu.full)
    grad_c_parts = contract_last(grad_up, wu_full)
    grad_c = scatter_rows(grad_c_parts)
    sum_wd.run(1)
    grad_c = then(grad_c, sum_wd)
    grad_gain2_part = jnp.sum(grad_c * normed_two, axis=0)
    grad_bias2_part = jnp.sum(grad_c, axis=0)
    grad_hidden = grad_out + norm_back(grad_c * gain_two, normed_two, inv_two)
    grad_attn_all = gather_rows(grad_hidden.astype(jnp.bfloat16))
    sum_wd.run(2)
    sum_wu.run(1)
    grad_attn_all = then(grad_attn_all, sum_wd, sum_wu)
    sum_wo = weight_grad(in_order(grad_attn_all), gated_out, False)
    grad_attn_all = tie(grad_attn_all, sum_wo.full)
    grad_gated = plain_dot(grad_attn_all, wo_full).reshape(seg_len, heads_local, DV)
    _, silu_pull = jax.vjp(jax.nn.silu, gate_pre)
    grad_gate = silu_pull((grad_gated * grouped).reshape(seg_len, heads_local * DV))[0].astype(
        jnp.bfloat16
    )
    retained_gradient = norm_back(grad_gated * gate_act, grouped, inv_group).astype(jnp.bfloat16)
    state_grad_own = jnp.einsum(
        "ybn,ybw->bnw",
        (rotated_queries.astype(jnp.float32) * continuation_factor[:, :, None]).astype(
            jnp.bfloat16
        ),
        retained_gradient,
        preferred_element_type=jnp.float32,
    )
    grad_slots = (group_onehot[:, None, None, None] * state_grad_own[None]).astype(jnp.bfloat16)
    grad_summed = ring_total(grad_slots.reshape(-1, DV)).reshape(grad_slots.shape)
    retained_gradient = tie(retained_gradient, grad_summed)
    sum_wu.run(2)
    a_order = in_order(a_all)
    grad_gate = then(grad_gate, sum_wu)
    sum_wg = weight_grad(a_order, grad_gate, True)
    retained_gradient = tie(retained_gradient, sum_wg.full)
    sum_wu.run(1)
    sum_wo.run(1)
    grad_weights = jnp.einsum(
        "thv,nhv->htn", retained_gradient, reduced_values, preferred_element_type=jnp.float32
    )
    grad_values = jnp.einsum(
        "htn,thv->nhv", weights_low, retained_gradient, preferred_element_type=jnp.float32
    )
    grad_scores = then((grad_weights * decay_mat).astype(jnp.bfloat16), sum_wu, sum_wo)
    sum_wo.run(1)
    grad_q_rot = jnp.einsum(
        "htn,nhk->thk", grad_scores, rotated_keys, preferred_element_type=jnp.float32
    )
    grad_q_rot = grad_q_rot + continuation_factor[:, :, None] * jnp.einsum(
        "mjr,jwr->mjw", retained_gradient, state_lookup, preferred_element_type=jnp.float32
    )
    grad_k_rot = jnp.einsum(
        "htn,thk->nhk", grad_scores, rotated_queries, preferred_element_type=jnp.float32
    )
    grad_queries = (
        rotate_back(grad_q_rot * q_scale, cosine, sine_tab, grow_fac)
        .reshape(seg_len, heads_local * DK)
        .astype(jnp.bfloat16)
    )
    grad_queries = then(grad_queries, sum_wo)
    sum_wq = weight_grad(a_order, grad_queries, False)
    state_gradient = (
        prompt_flag
        * jnp.sum(grad_summed.astype(jnp.float32) * group_onehot[:, None, None, None], axis=0)
    ).astype(jnp.bfloat16)
    grad_k_rot = grad_k_rot + state_weighting[:, :, None] * jnp.einsum(
        "ilm,lpm->ilp", reduced_values, state_gradient, preferred_element_type=jnp.float32
    )
    grad_values = grad_values + state_weighting[:, :, None] * jnp.einsum(
        "zdo,doi->zdi", rotated_keys, state_gradient, preferred_element_type=jnp.float32
    )
    grad_keys = (
        rotate_back(grad_k_rot, cosine, sine_tab, shrink)
        .reshape(seg_len, heads_local * DK)
        .astype(jnp.bfloat16)
    )
    grad_vlow = grad_values.reshape(seg_len, heads_local * DV).astype(jnp.bfloat16)
    sum_wv = weight_grad(a_order, grad_vlow, True)
    sum_wk = weight_grad(a_order, grad_keys, False)
    grad_keys = tie(grad_keys, (sum_wv.arrived, sum_wk.arrived))
    grad_a = scatter_rows(
        contract_last(grad_queries, wq_full)
        + contract_last(grad_gate, wg_full)
        + contract_last(grad_keys, wk_full)
        + contract_last(grad_vlow, wv_full)
    )
    sum_wo.run(2)
    sum_wg.run(1)
    grad_gain1_part = jnp.sum(grad_a * normed_one, axis=0)
    grad_bias1_part = jnp.sum(grad_a, axis=0)
    grad_tokens = grad_hidden + norm_back(grad_a * gain_one, normed_one, inv_one)

    sums = jnp.stack([grad_gain1_part, grad_bias1_part, grad_gain2_part, grad_bias2_part])
    totals = jnp.sum(exchange_blocks(packed(sums, squared_own)), axis=0)
    loss_value = totals[4, 0] / (valid_count * model_dim)
    key_width = w_key.shape[1]
    sum_wg.run(2)
    sum_wg.moving = [tie(x, totals) for x in sum_wg.moving]

    return (
        block_out,
        grad_tokens,
        loss_value,
        totals[0, :block],
        totals[1, :block],
        sum_wq.result(),
        sum_wk.result(),
        sum_wv.result(),
        sum_wg.result(),
        sum_wo.result(),
        totals[2, :block],
        totals[3, :block],
        sum_wu.result(),
        sum_wd.result(),
    )


def solution(mesh):
    return jax.shard_map(
        on_device,
        mesh=mesh,
        in_specs=(
            P(("dp", "mp"), None),
            P(("dp", "mp"), None),
            P("dp", "mp"),
            P(),
            P(),
            P("dp"),
            P("dp"),
            P("dp", "mp"),
            P("dp", "mp"),
            P("dp", "mp"),
            P("dp", "mp"),
            P("dp", "mp"),
            P("dp"),
            P("dp"),
            P("dp", "mp"),
            P("dp", "mp"),
        ),
        out_specs=(
            P(("dp", "mp"), None),
            P(("dp", "mp"), None),
            P(),
            P("dp"),
            P("dp"),
            P("dp", "mp"),
            P("dp", "mp"),
            P("dp", "mp"),
            P("dp", "mp"),
            P("dp", "mp"),
            P("dp"),
            P("dp"),
            P("dp", "mp"),
            P("dp", "mp"),
        ),
        check_vma=False,
    )
```
